512 devices in a mesh: row: 32 (over z_lo, x, core), col: 16 (over y, z_hi).
Axes of the slice: x: 4, y: 8, z: 8 (z_hi: 2, z_lo: 4; z = z_hi * 4 + z_lo), core: 2. Of those that a mesh axis runs over, the one named last changes fastest.
Arguments:
- halves: bfloat16 [96, 800, 800], P(None, 'row', 'col'), may hold values from -6 to 6
- first_factor: bfloat16 [4000, 800], P('col'), may hold values from -0.21875 to 0.21875
- second_factor: bfloat16 [4000, 800], P('col'), may hold values from -0.09375 to 0.09375
- weights: bfloat16 [4000, 96], P('col'), may hold values from 0.25 to 4
Outputs:
- cycle: bfloat16 [96, 800, 800], P('col', 'row')
The draws below stay inside these ranges and needn't reach their ends.
All inputs are finite; a program needn't handle non-finite values.
Results may differ from the reference program's by a relative error of at most 0.0095.
Values may be sent and summed in bfloat16 or wider, within the bound.
No kernel may reach another device: no remote copies, remote signals or barrier semaphores. Data moves between devices by JAX's collectives and lax.ppermute only.
A program may use at most 64 MiB of HBM per device.

```python
import math
import jax
import jax.numpy as jnp
from jax import lax

V = 800
NQ = 4000
O = 96
QB = 250


def steps_of(rng, shape, pieces, smallest, high):
    def one(dim, parts):
        heights = jax.random.uniform(jax.random.fold_in(jax.random.fold_in(rng, 6), dim), (parts,), jnp.float32, smallest / len(pieces), high / len(pieces))
        return jnp.repeat(jnp.exp(heights), shape[dim] // parts).reshape((-1,) + (1,) * (len(shape) - dim - 1))

    loudness = one(*pieces[0])
    for cut in pieces[1:]:
        loudness = loudness * one(*cut)
    return loudness


def bell_draw(rng, dims, spread, limit, shards=(), held_as=jnp.bfloat16):
    drawn = spread * jax.random.normal(rng, dims, jnp.float32)
    if shards:
        drawn = drawn * steps_of(rng, dims, shards, -0.22, 0.18)
    return jnp.clip(drawn, -limit, limit).astype(held_as)


def setup_inputs(seed: int = 0) -> dict:
    seeds = jax.random.split(jax.random.key(seed), 5)
    return {
        "halves": bell_draw(seeds[0], (O, V, V), 1.0, 6.0, ((1, 32), (2, 16))),
        "first_factor": bell_draw(seeds[1], (NQ, V), V ** -0.5, 0.21875, ((0, 16),)),
        "second_factor": bell_draw(seeds[2], (NQ, V), NQ ** -0.5, 0.09375, ((0, 16),)),
        "weights": jnp.clip(jnp.exp(math.log(4.0) - 2.7725887 * jax.random.uniform(seeds[3], (NQ, O), jnp.float32) ** steps_of(seeds[3], (NQ, O), ((0, 16),), -0.2, 0.2)), 0.25, 4.0).astype(jnp.bfloat16),
    }


def reference(halves, first_factor, second_factor, weights):
    block_count = NQ // QB
    right_blocks = second_factor.reshape(block_count, QB, V).astype(jnp.float32)

    def one_orbital(index):
        sheet = lax.dynamic_index_in_dim(halves, index, 0, keepdims=False)
        amplitude = (sheet.astype(jnp.float32) - sheet.T.astype(jnp.float32)).astype(jnp.bfloat16)
        scale = lax.dynamic_index_in_dim(weights, index, 1, keepdims=False).astype(jnp.float32)
        scaled = (jnp.dot(amplitude, first_factor.T, preferred_element_type=jnp.float32) * scale[None, :]).astype(jnp.bfloat16)
        blocks = jnp.einsum("akq,kqc->kac", scaled.reshape(V, block_count, QB).astype(jnp.float32), right_blocks)
        blocks = lax.optimization_barrier(blocks.astype(jnp.bfloat16)).astype(jnp.float32)
        return jnp.sum(blocks, axis=0).astype(jnp.bfloat16)

    return lax.map(one_orbital, jnp.arange(O, dtype=jnp.int32))
```

```python
import functools

import jax
import jax.numpy as jnp
from jax import lax
from jax.experimental import pallas as pl
from jax.experimental.pallas import tpu as pltpu
from jax.sharding import Mesh, PartitionSpec as P

ROWS, SLOT, LANES = 25, 32, 128


def amplitude_kernel(direct_ref, mirrored_ref, out_ref):
    count = mirrored_ref.shape[0]
    mirrored = mirrored_ref[...].astype(jnp.float32).reshape(count * SLOT, LANES)
    mirrored = jnp.transpose(mirrored)
    lane = lax.broadcasted_iota(jnp.int32, (SLOT, LANES), 1) // SLOT
    for quad in range(count // 4):
        parts = [direct_ref[quad, k].astype(jnp.float32) for k in range(4)]
        for orbital in range(4):
            direct = None
            for k in range(4):
                shift = SLOT * ((k - orbital) % 4)
                moved = pltpu.roll(parts[k], shift, 1) if shift else parts[k]
                direct = moved if direct is None else jnp.where(lane == k, moved, direct)
            rows = slice(orbital * SLOT, (orbital + 1) * SLOT)
            columns = slice(quad * LANES, (quad + 1) * LANES)
            out_ref[rows, columns] = (direct - mirrored[rows, columns]).astype(out_ref.dtype)


def contraction_kernel(where_ref, amplitude_ref, factors_ref, own_ref, other_ref, total_ref, *, orbitals):
    step = pl.program_id(0)
    rows, depth = amplitude_ref.shape
    virtual = own_ref.shape[1]
    pick = lax.broadcasted_iota(jnp.int32, (rows, orbitals), 0) // SLOT + where_ref[0]
    pick = (pick == lax.broadcasted_iota(jnp.int32, (rows, orbitals), 1)).astype(jnp.bfloat16)
    scaled = jnp.dot(amplitude_ref[...], factors_ref[0, :depth], preferred_element_type=jnp.float32)
    scale = jnp.dot(pick, factors_ref[0, depth : depth + orbitals], preferred_element_type=jnp.float32)
    scaled = (scaled * scale).astype(jnp.bfloat16)
    part = lax.dot_general(
        scaled, factors_ref[0, depth + orbitals :], (((1,), (1,)), ((), ())), preferred_element_type=jnp.float32
    )

    @pl.when(step == 0)
    def _():
        total_ref[...] = part

    @pl.when(step > 0)
    def _():
        total_ref[...] += part

    @pl.when(step == pl.num_programs(0) - 1)
    def _():
        half = rows // 2
        mine = where_ref[1]
        own_ref[...] = total_ref[pl.ds(pl.multiple_of(mine * half, half), half), :]
        other_ref[...] = total_ref[pl.ds(pl.multiple_of((1 - mine) * half, half), half), :].astype(other_ref.dtype)


def body(halves, first_factor, second_factor, weights):
    y_count, row_count = lax.axis_size("y"), lax.axis_size("p") * 2
    orbitals, block = halves.shape[0], first_factor.shape[0]
    virtual = first_factor.shape[1]
    local = orbitals // y_count
    groups = local // 4
    y, zh, core = lax.axis_index("y"), lax.axis_index("zh"), lax.axis_index("c")

    lanes = (block + LANES - 1) // LANES * LANES
    widen = ((0, 0), (0, lanes - block))
    first = jnp.pad(first_factor.T.reshape(row_count, ROWS, block), ((0, 0), (0, SLOT - ROWS), (0, lanes - block)))
    packed = jnp.concatenate(
        [first.reshape(row_count * SLOT, lanes), jnp.pad(weights.T, widen), jnp.pad(second_factor.T, widen)]
    )
    half = packed.shape[0] // 2
    share = lax.dynamic_slice_in_dim(packed, core * half, half, 0)
    factors = lax.all_gather(share, ("y", "c"), axis=0, tiled=True).reshape(y_count, 2 * half, lanes)

    pieces = halves.reshape(y_count, groups, 4, ROWS, 2, ROWS).transpose(0, 4, 1, 3, 2, 5)
    slack = (0, SLOT - ROWS)
    pieces = jnp.pad(pieces, ((0, 0), (0, 0), (0, 0), slack, (0, 0), slack))
    pieces = pieces.reshape(y_count, 1, 2, groups * SLOT, LANES)
    pieces = jnp.broadcast_to(pieces, (y_count, 2, 2, groups * SLOT, LANES)).reshape(2 * y_count, 2, groups * SLOT, LANES)
    direct = lax.all_to_all(pieces, ("y", "zh"), 0, 0, tiled=True).reshape(row_count, groups * SLOT, LANES)
    mirrored = lax.all_to_all(direct, ("p", "c"), 0, 0, tiled=True)
    amplitude = pl.pallas_call(
        amplitude_kernel,
        grid=(groups,),
        in_specs=[
            pl.BlockSpec((row_count // 4, 4, SLOT, LANES), lambda g: (0, 0, g, 0)),
            pl.BlockSpec((row_count, SLOT, LANES), lambda g: (0, g, 0)),
        ],
        out_specs=pl.BlockSpec((LANES, row_count * SLOT), lambda g: (g, 0)),
        out_shape=jax.ShapeDtypeStruct((groups * LANES, row_count * SLOT), jnp.bfloat16),
        name="amplitude",
    )(direct.reshape(row_count // 4, 4, groups * SLOT, LANES), mirrored)

    rows = local * SLOT
    where = jnp.stack([y * local, zh])
    own, other = pl.pallas_call(
        functools.partial(contraction_kernel, orbitals=orbitals),
        grid=(y_count,),
        in_specs=[
            pl.BlockSpec(memory_space=pltpu.SMEM),
            pl.BlockSpec((rows, row_count * SLOT), lambda k: (0, 0)),
            pl.BlockSpec((1, 2 * half, lanes), lambda k: (k, 0, 0)),
        ],
        out_specs=[pl.BlockSpec((rows // 2, virtual), lambda k: (0, 0))] * 2,
        out_shape=[
            jax.ShapeDtypeStruct((rows // 2, virtual), jnp.float32),
            jax.ShapeDtypeStruct((rows // 2, virtual), jnp.bfloat16),
        ],
        scratch_shapes=[pltpu.VMEM((rows, virtual), jnp.float32)],
        name="contraction",
    )(where, amplitude, factors)
    received = lax.ppermute(other, "zh", [(0, 1), (1, 0)])
    cycle = (own + received.astype(jnp.float32)).astype(jnp.bfloat16)
    return cycle.reshape(local // 2, SLOT, virtual)[:, :ROWS]


def solution(mesh):
    rows, columns = mesh.devices.shape
    fine = Mesh(mesh.devices.reshape(rows // 2, 2, columns // 2, 2), ("p", "c", "y", "zh"))
    row, col = ("p", "c"), ("y", "zh")
    placed = (P(None, row, col), P(col, None), P(col, None), P(col, None))
    return jax.shard_map(body, mesh=fine, in_specs=placed, out_specs=P(col, row, None), check_vma=False)
```

```python
import functools

import jax
import jax.numpy as jnp
from jax import lax
from jax.experimental import pallas as pl
from jax.experimental.pallas import tpu as pltpu
from jax.sharding import Mesh, PartitionSpec as P

ROWS, SLOT, LANES = 25, 32, 128
F32, BF16 = jnp.float32, jnp.bfloat16


def pack_kernel(core_ref, first_hbm, weights_hbm, second_hbm, out_ref, held, sems):
    virtual, block = first_hbm.shape
    half = weights_hbm.shape[0] // 2
    out_ref[:, LANES:] = jnp.zeros((out_ref.shape[0], out_ref.shape[1] - LANES), BF16)

    @pl.when(core_ref[0] == 0)
    def _():
        big = pltpu.make_async_copy(first_hbm, held.at[pl.ds(0, virtual)], sems.at[0])
        small = pltpu.make_async_copy(weights_hbm.at[pl.ds(0, half)], held.at[pl.ds(virtual, half)], sems.at[1])
        big.start()
        small.start()
        big.wait()
        small.wait()

    @pl.when(core_ref[0] != 0)
    def _():
        small = pltpu.make_async_copy(weights_hbm.at[pl.ds(half, half)], held.at[pl.ds(0, half)], sems.at[1])
        big = pltpu.make_async_copy(second_hbm, held.at[pl.ds(half, virtual)], sems.at[0])
        big.start()
        small.start()
        big.wait()
        small.wait()

    out_ref[:, :block] = held[...]


def direct_kernel(pieces_ref, out_ref, wide_ref, pick_ref):
    count = pieces_ref.shape[0]
    groups = out_ref.shape[0] // LANES
    depth, width = pick_ref.shape
    at = lax.broadcasted_iota(jnp.int32, (depth, width), 0)
    to = lax.broadcasted_iota(jnp.int32, (depth, width), 1)
    within = at % SLOT
    target = jnp.where(within < ROWS, (at // SLOT) * ROWS + within, -1)
    pick_ref[...] = jnp.where(target == to, 1.0, 0.0).astype(BF16)
    lane = lax.broadcasted_iota(jnp.int32, (ROWS, LANES), 1) // SLOT
    wide_ref[...] = jnp.zeros_like(wide_ref)
    for quad in range(count // 4):
        whole = [pieces_ref[4 * quad + k].astype(F32) for k in range(4)]
        for group in range(groups):
            parts = [w[group * ROWS : (group + 1) * ROWS] for w in whole]
            for orbital in range(4):
                placed = None
                for k in range(4):
                    shift = SLOT * ((k - orbital) % 4)
                    moved = pltpu.roll(parts[k], shift, 1) if shift else parts[k]
                    placed = moved if placed is None else jnp.where(lane == k, moved, placed)
                row = (4 * group + orbital) * SLOT
                wide_ref[row : row + ROWS, quad * LANES : (quad + 1) * LANES] = placed
    out_ref[...] = jnp.dot(wide_ref[...].astype(BF16), pick_ref[...], preferred_element_type=F32).astype(BF16)


def amplitude_kernel(direct_ref, pieces_ref, out_ref, flat_ref):
    count = pieces_ref.shape[0]
    groups = out_ref.shape[0] // LANES
    for source in range(count):
        whole = pieces_ref[source].astype(F32)
        for group in range(groups):
            flat_ref[group, source * ROWS : (source + 1) * ROWS, :] = whole[group * ROWS : (group + 1) * ROWS]
    for group in range(groups):
        rows = slice(group * LANES, (group + 1) * LANES)
        mirrored = jnp.transpose(flat_ref[group])
        out_ref[rows, :] = (direct_ref[rows, :].astype(F32) - mirrored).astype(BF16)


def contraction_kernel(where_ref, amplitude_ref, factors_hbm, own_ref, other_ref, held, total_ref, sems, *, orbitals):
    rows, depth = amplitude_ref.shape
    chunks = sems.shape[0]
    per = factors_hbm.shape[0] // chunks
    copies = [
        pltpu.make_async_copy(factors_hbm.at[pl.ds(j * per, per)], held.at[pl.ds(j * per, per)], sems.at[j])
        for j in range(chunks)
    ]
    for copy in copies:
        copy.start()
    pick = lax.broadcasted_iota(jnp.int32, (rows, orbitals), 0) // SLOT + where_ref[0]
    pick = (pick == lax.broadcasted_iota(jnp.int32, (rows, orbitals), 1)).astype(BF16)
    amplitude = amplitude_ref[...]
    total = None
    for j in range(chunks):
        copies[j].wait()
        scaled, second = [], []
        for k in range(j * per, (j + 1) * per):
            value = jnp.dot(amplitude, held[k, :depth], preferred_element_type=F32)
            scale = jnp.dot(pick, held[k, depth : depth + orbitals], preferred_element_type=F32)
            scaled.append((value * scale).astype(BF16))
            second.append(held[k, depth + orbitals :])
        part = lax.dot_general(
            jnp.concatenate(scaled, 1), jnp.concatenate(second, 1), (((1,), (1,)), ((), ())), preferred_element_type=F32
        )
        total = part if total is None else total + part
    total_ref[...] = total
    half = rows // 2
    mine = where_ref[1]
    own_ref[...] = total_ref[pl.ds(pl.multiple_of(mine * half, half), half), :]
    other = total_ref[pl.ds(pl.multiple_of((1 - mine) * half, half), half), :]
    other = [other[k * SLOT : k * SLOT + ROWS] for k in range(half // SLOT)]
    other_ref[...] = jnp.concatenate(other, 0).astype(BF16)


def finish_kernel(own_ref, received_ref, out_ref):
    received = received_ref[...].astype(F32)
    for k in range(out_ref.shape[0]):
        out_ref[k] = (own_ref[k * SLOT : k * SLOT + ROWS] + received[k * ROWS : (k + 1) * ROWS]).astype(BF16)


def vmem(count):
    return [pl.BlockSpec(memory_space=pltpu.VMEM)] * count


def hbm(count):
    return [pl.BlockSpec(memory_space=pl.ANY)] * count


SMEM = [pl.BlockSpec(memory_space=pltpu.SMEM)]
ROOM = pltpu.CompilerParams(vmem_limit_bytes=32 * 2**20)
SMALL = pltpu.CompilerParams(vmem_limit_bytes=16 * 2**20)


def body(halves, first_factor, second_factor, weights):
    y_count, row_count = lax.axis_size("y"), lax.axis_size("p") * 2
    orbitals = halves.shape[0]
    block, virtual = first_factor.shape
    local = orbitals // y_count
    groups = local // 4
    y, zh, core = lax.axis_index("y"), lax.axis_index("zh"), lax.axis_index("c")

    lanes = (block + LANES - 1) // LANES * LANES
    half = virtual + orbitals // 2
    share = pl.pallas_call(
        pack_kernel,
        in_specs=SMEM + hbm(3),
        out_specs=vmem(1)[0],
        out_shape=jax.ShapeDtypeStruct((half, lanes), BF16),
        scratch_shapes=[pltpu.VMEM((half, block), BF16), pltpu.SemaphoreType.DMA((2,))],
        compiler_params=SMALL,
        name="pack",
    )(core.reshape(1), first_factor.T, weights.T, second_factor.T)
    factors = lax.all_gather(share, ("y", "c"), axis=0, tiled=True).reshape(y_count, 2 * half, lanes)

    used = groups * ROWS
    piece = (used + 15) // 16 * 16
    pieces = halves.reshape(y_count, groups, 4, ROWS, 2, ROWS).transpose(0, 4, 1, 3, 2, 5)
    pieces = jnp.pad(pieces, ((0, 0),) * 5 + ((0, SLOT - ROWS),)).reshape(y_count, 1, 2, used, LANES)
    pieces = jnp.pad(pieces, ((0, 0),) * 3 + ((0, piece - used), (0, 0)))
    pieces = jnp.broadcast_to(pieces, (y_count, 2, 2, piece, LANES)).reshape(2 * y_count, 2, piece, LANES)
    direct = lax.all_to_all(pieces, ("y", "zh"), 0, 0, tiled=True).reshape(row_count, piece, LANES)
    mirrored = lax.all_to_all(direct, ("p", "c"), 0, 0, tiled=True)
    rows = local * SLOT
    laid = jax.ShapeDtypeStruct((rows, virtual), BF16)
    direct = pl.pallas_call(
        direct_kernel,
        in_specs=vmem(1),
        out_specs=vmem(1)[0],
        out_shape=laid,
        scratch_shapes=[pltpu.VMEM((rows, row_count * SLOT), F32), pltpu.VMEM((row_count * SLOT, virtual), BF16)],
        compiler_params=ROOM,
        cost_estimate=pl.CostEstimate(flops=2 * rows * row_count * SLOT * virtual, bytes_accessed=4 * rows * virtual, transcendentals=0),
        name="direct",
    )(direct)
    amplitude = pl.pallas_call(
        amplitude_kernel,
        in_specs=vmem(2),
        out_specs=vmem(1)[0],
        out_shape=laid,
        scratch_shapes=[pltpu.VMEM((groups, virtual, LANES), F32)],
        compiler_params=ROOM,
        name="amplitude",
    )(direct, mirrored)

    kept = rows // 2
    sent = local // 2 * ROWS
    chunks = max(y_count // 2, 1)
    own, other = pl.pallas_call(
        functools.partial(contraction_kernel, orbitals=orbitals),
        in_specs=SMEM + vmem(1) + hbm(1),
        out_specs=vmem(2),
        out_shape=[jax.ShapeDtypeStruct((kept, virtual), F32), jax.ShapeDtypeStruct((sent, virtual), BF16)],
        scratch_shapes=[
            pltpu.VMEM((y_count, 2 * half, lanes), BF16),
            pltpu.VMEM((rows, virtual), F32),
            pltpu.SemaphoreType.DMA((chunks,)),
        ],
        compiler_params=ROOM,
        name="contraction",
    )(jnp.stack([y * local, zh]), amplitude, factors)
    received = lax.ppermute(other, "zh", [(0, 1), (1, 0)])
    return pl.pallas_call(
        finish_kernel,
        in_specs=vmem(2),
        out_specs=vmem(1)[0],
        out_shape=jax.ShapeDtypeStruct((local // 2, ROWS, virtual), BF16),
        compiler_params=SMALL,
        name="finish",
    )(own, received)


def solution(mesh):
    rows, columns = mesh.devices.shape
    fine = Mesh(mesh.devices.reshape(rows // 2, 2, columns // 2, 2), ("p", "c", "y", "zh"))
    row, col = ("p", "c"), ("y", "zh")
    placed = (P(None, row, col), P(col, None), P(col, None), P(col, None))
    return jax.shard_map(body, mesh=fine, in_specs=placed, out_specs=P(col, row, None), check_vma=False)
```

```python
import functools

import jax
import jax.numpy as jnp
from jax import lax
from jax.experimental import pallas as pl
from jax.experimental.pallas import tpu as pltpu
from jax.sharding import Mesh, PartitionSpec as P

ROWS, SLOT, LANES = 25, 32, 128
F32, BF16 = jnp.float32, jnp.bfloat16


def pack_kernel(part_ref, first_hbm, weights_hbm, second_hbm, out_ref, held, sems):
    virtual, block = first_hbm.shape
    orbitals = weights_hbm.shape[0]
    rows = out_ref.shape[0]
    used = 2 * virtual + orbitals
    sources = ((first_hbm, 0, virtual), (weights_hbm, virtual, orbitals), (second_hbm, virtual + orbitals, virtual))
    copies = [
        pltpu.make_async_copy(ref, held.at[pl.ds(start, size)], sems.at[j]) for j, (ref, start, size) in enumerate(sources)
    ]
    for copy in copies:
        copy.start()
    if held.shape[0] > used:
        held[used:, :] = jnp.zeros((held.shape[0] - used, block), BF16)
    out_ref[:, LANES:] = jnp.zeros((rows, out_ref.shape[1] - LANES), BF16)
    for copy in copies:
        copy.wait()
    out_ref[:, :block] = held[pl.ds(pl.multiple_of(part_ref[0] * rows, rows), rows), :]


def direct_kernel(pieces_ref, out_ref, wide_ref, pick_ref):
    count = pieces_ref.shape[0]
    orbitals = out_ref.shape[0] // SLOT
    groups = -(-orbitals // 4)
    depth, width = pick_ref.shape
    at = lax.broadcasted_iota(jnp.int32, (depth, width), 0)
    to = lax.broadcasted_iota(jnp.int32, (depth, width), 1)
    within = at % SLOT
    target = jnp.where(within < ROWS, (at // SLOT) * ROWS + within, -1)
    pick_ref[...] = jnp.where(target == to, 1.0, 0.0).astype(BF16)
    lane = lax.broadcasted_iota(jnp.int32, (ROWS, LANES), 1) // SLOT
    wide_ref[...] = jnp.zeros_like(wide_ref)
    for quad in range(count // 4):
        whole = [pieces_ref[4 * quad + k].astype(F32) for k in range(4)]
        for group in range(groups):
            parts = [w[group * ROWS : (group + 1) * ROWS] for w in whole]
            for orbital in range(min(4, orbitals - 4 * group)):
                placed = None
                for k in range(4):
                    shift = SLOT * ((k - orbital) % 4)
                    moved = pltpu.roll(parts[k], shift, 1) if shift else parts[k]
                    placed = moved if placed is None else jnp.where(lane == k, moved, placed)
                row = (4 * group + orbital) * SLOT
                wide_ref[row : row + ROWS, quad * LANES : (quad + 1) * LANES] = placed
    out_ref[...] = jnp.dot(wide_ref[...].astype(BF16), pick_ref[...], preferred_element_type=F32).astype(BF16)


def amplitude_kernel(direct_ref, pieces_ref, out_ref, flat_ref):
    count = pieces_ref.shape[0]
    orbitals = out_ref.shape[0] // SLOT
    groups = -(-orbitals // 4)
    for source in range(count):
        whole = pieces_ref[source].astype(F32)
        for group in range(groups):
            flat_ref[group, source * ROWS : (source + 1) * ROWS, :] = whole[group * ROWS : (group + 1) * ROWS]
    for group in range(groups):
        count = min(4, orbitals - 4 * group) * SLOT
        rows = slice(group * LANES, group * LANES + count)
        mirrored = jnp.transpose(flat_ref[group])[:count]
        out_ref[rows, :] = (direct_ref[rows, :].astype(F32) - mirrored).astype(BF16)


def contraction_kernel(where_ref, amplitude_ref, factors_hbm, out_ref, held, sems, *, orbitals):
    rows, depth = amplitude_ref.shape
    chunks = sems.shape[0]
    per = factors_hbm.shape[0] // chunks
    copies = [
        pltpu.make_async_copy(factors_hbm.at[pl.ds(j * per, per)], held.at[pl.ds(j * per, per)], sems.at[j])
        for j in range(chunks)
    ]
    for copy in copies:
        copy.start()
    pick = lax.broadcasted_iota(jnp.int32, (rows, orbitals), 0) // SLOT + where_ref[0]
    pick = (pick == lax.broadcasted_iota(jnp.int32, (rows, orbitals), 1)).astype(BF16)
    amplitude = amplitude_ref[...]
    total = None
    for j in range(chunks):
        copies[j].wait()
        scaled, second = [], []
        for k in range(j * per, (j + 1) * per):
            value = jnp.dot(amplitude, held[k, :depth], preferred_element_type=F32)
            scale = jnp.dot(pick, held[k, depth : depth + orbitals], preferred_element_type=F32)
            scaled.append((value * scale).astype(BF16))
            second.append(held[k, depth + orbitals : 2 * depth + orbitals])
        part = lax.dot_general(
            jnp.concatenate(scaled, 1), jnp.concatenate(second, 1), (((1,), (1,)), ((), ())), preferred_element_type=F32
        )
        total = part if total is None else total + part
    for k in range(out_ref.shape[0]):
        out_ref[k] = total[k * SLOT : k * SLOT + ROWS].astype(BF16)


def vmem(count):
    return [pl.BlockSpec(memory_space=pltpu.VMEM)] * count


def hbm(count):
    return [pl.BlockSpec(memory_space=pl.ANY)] * count


SMEM = [pl.BlockSpec(memory_space=pltpu.SMEM)]
ROOM = pltpu.CompilerParams(vmem_limit_bytes=32 * 2**20)
FULL = pltpu.CompilerParams(vmem_limit_bytes=60 * 2**20)


def body(halves, first_factor, second_factor, weights):
    blocks, row_count = lax.axis_size("y") * lax.axis_size("zh"), lax.axis_size("zl") * lax.axis_size("x") * 2
    orbitals = halves.shape[0]
    block, virtual = first_factor.shape
    local = orbitals // blocks
    groups = -(-local // 4)
    column = lax.axis_index(("y", "zh"))

    lanes = -(-block // LANES) * LANES
    parts = lax.axis_size("zl") * 2
    height = -(-(2 * virtual + orbitals) // (16 * parts)) * 16
    share = pl.pallas_call(
        pack_kernel,
        in_specs=SMEM + hbm(3),
        out_specs=vmem(1)[0],
        out_shape=jax.ShapeDtypeStruct((height, lanes), BF16),
        scratch_shapes=[pltpu.VMEM((parts * height, block), BF16), pltpu.SemaphoreType.DMA((3,))],
        compiler_params=FULL,
        name="pack",
    )(lax.axis_index(("zl", "c")).reshape(1), first_factor.T, weights.T, second_factor.T)
    factors = lax.all_gather(share, ("y", "zh", "zl", "c"), axis=0, tiled=True).reshape(blocks, parts * height, lanes)

    used = groups * ROWS
    piece = -(-used // 16) * 16
    pieces = halves.reshape(blocks, local, ROWS, 2, ROWS)
    pieces = jnp.pad(pieces, ((0, 0), (0, 4 * groups - local), (0, 0), (0, 0), (0, 0)))
    pieces = pieces.reshape(blocks, groups, 4, ROWS, 2, ROWS).transpose(0, 4, 1, 3, 2, 5)
    pieces = jnp.pad(pieces, ((0, 0),) * 5 + ((0, SLOT - ROWS),)).reshape(blocks, 2, used, LANES)
    pieces = jnp.pad(pieces, ((0, 0), (0, 0), (0, piece - used), (0, 0)))
    direct = lax.all_to_all(pieces, ("y", "zh"), 0, 0, tiled=True).reshape(row_count, piece, LANES)
    mirrored = lax.all_to_all(direct, ("zl", "x", "c"), 0, 0, tiled=True)
    rows = local * SLOT
    laid = jax.ShapeDtypeStruct((rows, virtual), BF16)
    direct = pl.pallas_call(
        direct_kernel,
        in_specs=vmem(1),
        out_specs=vmem(1)[0],
        out_shape=laid,
        scratch_shapes=[pltpu.VMEM((rows, row_count * SLOT), F32), pltpu.VMEM((row_count * SLOT, virtual), BF16)],
        compiler_params=ROOM,
        cost_estimate=pl.CostEstimate(flops=2 * rows * row_count * SLOT * virtual, bytes_accessed=4 * rows * virtual, transcendentals=0),
        name="direct",
    )(direct)
    amplitude = pl.pallas_call(
        amplitude_kernel,
        in_specs=vmem(2),
        out_specs=vmem(1)[0],
        out_shape=laid,
        scratch_shapes=[pltpu.VMEM((groups, virtual, LANES), F32)],
        compiler_params=ROOM,
        name="amplitude",
    )(direct, mirrored)

    chunks = blocks // 2
    return pl.pallas_call(
        functools.partial(contraction_kernel, orbitals=orbitals),
        in_specs=SMEM + vmem(1) + hbm(1),
        out_specs=vmem(1)[0],
        out_shape=jax.ShapeDtypeStruct((local, ROWS, virtual), BF16),
        scratch_shapes=[pltpu.VMEM((blocks, parts * height, lanes), BF16), pltpu.SemaphoreType.DMA((chunks,))],
        compiler_params=FULL,
        name="contraction",
    )((column * local).reshape(1), amplitude, factors)


def solution(mesh):
    rows, columns = mesh.devices.shape
    along_x = 4 if rows % 32 == 0 else 2
    shape = (rows // (2 * along_x), along_x, 2, columns // 2, 2)
    fine = Mesh(mesh.devices.reshape(shape), ("zl", "x", "c", "y", "zh"))
    row, col = ("zl", "x", "c"), ("y", "zh")
    placed = (P(None, row, col), P(col, None), P(col, None), P(col, None))
    return jax.shard_map(body, mesh=fine, in_specs=placed, out_specs=P(col, row, None), check_vma=False)
```

```python
import functools

import jax
import jax.numpy as jnp
from jax import lax
from jax.experimental import pallas as pl
from jax.experimental.pallas import tpu as pltpu
from jax.sharding import Mesh, PartitionSpec as P

ROWS, SLOT, LANES = 25, 32, 128
F32, BF16 = jnp.float32, jnp.bfloat16


def pack_kernel(part_ref, first_hbm, weights_hbm, second_hbm, out_ref, held, sems):
    virtual, block = first_hbm.shape
    orbitals = weights_hbm.shape[0]
    rows = out_ref.shape[0]
    used = 2 * virtual + orbitals
    sources = ((first_hbm, 0, virtual), (weights_hbm, virtual, orbitals), (second_hbm, virtual + orbitals, virtual))
    copies = [
        pltpu.make_async_copy(ref, held.at[pl.ds(start, size)], sems.at[j]) for j, (ref, start, size) in enumerate(sources)
    ]
    for copy in copies:
        copy.start()
    if held.shape[0] > used:
        held[used:, :] = jnp.zeros((held.shape[0] - used, block), BF16)
    out_ref[:, LANES:] = jnp.zeros((rows, out_ref.shape[1] - LANES), BF16)
    for copy in copies:
        copy.wait()
    out_ref[:, :block] = held[pl.ds(pl.multiple_of(part_ref[0] * rows, rows), rows), :]


def direct_kernel(pieces_ref, out_ref, wide_ref, pick_ref):
    count = pieces_ref.shape[0]
    groups = out_ref.shape[0] // LANES
    depth, width = pick_ref.shape
    at = lax.broadcasted_iota(jnp.int32, (depth, width), 0)
    to = lax.broadcasted_iota(jnp.int32, (depth, width), 1)
    within = at % SLOT
    target = jnp.where(within < ROWS, (at // SLOT) * ROWS + within, -1)
    pick_ref[...] = jnp.where(target == to, 1.0, 0.0).astype(BF16)
    lane = lax.broadcasted_iota(jnp.int32, (ROWS, LANES), 1) // SLOT
    wide_ref[...] = jnp.zeros_like(wide_ref)
    for quad in range(count // 4):
        whole = [pieces_ref[4 * quad + k].astype(F32) for k in range(4)]
        for group in range(groups):
            parts = [w[group * ROWS : (group + 1) * ROWS] for w in whole]
            for orbital in range(4):
                placed = None
                for k in range(4):
                    shift = SLOT * ((k - orbital) % 4)
                    moved = pltpu.roll(parts[k], shift, 1) if shift else parts[k]
                    placed = moved if placed is None else jnp.where(lane == k, moved, placed)
                row = (4 * group + orbital) * SLOT
                wide_ref[row : row + ROWS, quad * LANES : (quad + 1) * LANES] = placed
    out_ref[...] = jnp.dot(wide_ref[...].astype(BF16), pick_ref[...], preferred_element_type=F32).astype(BF16)


def amplitude_kernel(direct_ref, pieces_ref, out_ref, flat_ref):
    count = pieces_ref.shape[0]
    groups = out_ref.shape[0] // LANES
    for source in range(count):
        whole = pieces_ref[source].astype(F32)
        for group in range(groups):
            flat_ref[group, source * ROWS : (source + 1) * ROWS, :] = whole[group * ROWS : (group + 1) * ROWS]
    for group in range(groups):
        rows = slice(group * LANES, (group + 1) * LANES)
        mirrored = jnp.transpose(flat_ref[group])
        out_ref[rows, :] = (direct_ref[rows, :].astype(F32) - mirrored).astype(BF16)


def contraction_kernel(where_ref, amplitude_ref, factors_hbm, out_ref, held, sems, *, orbitals, swapped):
    depth = amplitude_ref.shape[1]
    rows = amplitude_ref.shape[0] // 2
    chunks = sems.shape[0]
    per = factors_hbm.shape[0] // chunks
    copies = [
        pltpu.make_async_copy(factors_hbm.at[pl.ds(j * per, per)], held.at[pl.ds(j * per, per)], sems.at[j])
        for j in range(chunks)
    ]
    for copy in copies:
        copy.start()
    side = 1 - where_ref[1] if swapped else where_ref[1]
    start = where_ref[0] + side * (rows // SLOT)
    pick = lax.broadcasted_iota(jnp.int32, (rows, orbitals), 0) // SLOT + start
    pick = (pick == lax.broadcasted_iota(jnp.int32, (rows, orbitals), 1)).astype(BF16)
    amplitude = amplitude_ref[pl.ds(pl.multiple_of(side * rows, rows), rows), :]
    total = None
    for j in range(chunks):
        copies[j].wait()
        scaled, second = [], []
        for k in range(j * per, (j + 1) * per):
            value = jnp.dot(amplitude, held[k, :depth], preferred_element_type=F32)
            scale = jnp.dot(pick, held[k, depth : depth + orbitals], preferred_element_type=F32)
            scaled.append((value * scale).astype(BF16))
            second.append(held[k, depth + orbitals : 2 * depth + orbitals])
        part = lax.dot_general(
            jnp.concatenate(scaled, 1), jnp.concatenate(second, 1), (((1,), (1,)), ((), ())), preferred_element_type=F32
        )
        total = part if total is None else total + part
    kept = [total[k * SLOT : k * SLOT + ROWS] for k in range(rows // SLOT)]
    out_ref[...] = jnp.concatenate(kept, 0).astype(out_ref.dtype)


def finish_kernel(own_ref, received_ref, out_ref):
    received = received_ref[...].astype(F32)
    for k in range(out_ref.shape[0]):
        rows = slice(k * ROWS, (k + 1) * ROWS)
        out_ref[k] = (own_ref[rows] + received[rows]).astype(BF16)


def vmem(count):
    return [pl.BlockSpec(memory_space=pltpu.VMEM)] * count


def hbm(count):
    return [pl.BlockSpec(memory_space=pltpu.HBM)] * count


SMEM = [pl.BlockSpec(memory_space=pltpu.SMEM)]
ROOM = pltpu.CompilerParams(vmem_limit_bytes=32 * 2**20)
SMALL = pltpu.CompilerParams(vmem_limit_bytes=16 * 2**20)
BIG = pltpu.CompilerParams(vmem_limit_bytes=48 * 2**20)
FULL = pltpu.CompilerParams(vmem_limit_bytes=60 * 2**20)


def body(halves, first_factor, second_factor, weights):
    y_count, row_count = lax.axis_size("y"), lax.axis_size("p") * 2
    orbitals = halves.shape[0]
    block, virtual = first_factor.shape
    local = orbitals // y_count
    groups = local // 4
    y, zh, core = lax.axis_index("y"), lax.axis_index("zh"), lax.axis_index("c")

    lanes = (block + LANES - 1) // LANES * LANES
    half = (virtual + orbitals // 2 + 15) // 16 * 16
    share = pl.pallas_call(
        pack_kernel,
        in_specs=SMEM + hbm(3),
        out_specs=vmem(1)[0],
        out_shape=jax.ShapeDtypeStruct((half, lanes), BF16),
        scratch_shapes=[pltpu.VMEM((2 * half, block), BF16), pltpu.SemaphoreType.DMA((3,))],
        compiler_params=FULL,
        name="pack",
    )(core.reshape(1), first_factor.T, weights.T, second_factor.T)
    factors = lax.all_gather(share, ("y", "c"), axis=0, tiled=True).reshape(y_count, 2 * half, lanes)

    used = groups * ROWS
    piece = (used + 15) // 16 * 16
    pieces = halves.reshape(y_count, groups, 4, ROWS, 2, ROWS).transpose(0, 4, 1, 3, 2, 5)
    pieces = jnp.pad(pieces, ((0, 0),) * 5 + ((0, SLOT - ROWS),)).reshape(y_count, 1, 2, used, LANES)
    pieces = jnp.pad(pieces, ((0, 0),) * 3 + ((0, piece - used), (0, 0)))
    pieces = jnp.broadcast_to(pieces, (y_count, 2, 2, piece, LANES)).reshape(2 * y_count, 2, piece, LANES)
    direct = lax.all_to_all(pieces, ("y", "zh"), 0, 0, tiled=True).reshape(row_count, piece, LANES)
    mirrored = lax.all_to_all(direct, ("p", "c"), 0, 0, tiled=True)
    rows = local * SLOT
    laid = jax.ShapeDtypeStruct((rows, virtual), BF16)
    direct = pl.pallas_call(
        direct_kernel,
        in_specs=vmem(1),
        out_specs=vmem(1)[0],
        out_shape=laid,
        scratch_shapes=[pltpu.VMEM((rows, row_count * SLOT), F32), pltpu.VMEM((row_count * SLOT, virtual), BF16)],
        compiler_params=ROOM,
        cost_estimate=pl.CostEstimate(flops=2 * rows * row_count * SLOT * virtual, bytes_accessed=4 * rows * virtual, transcendentals=0),
        name="direct",
    )(direct)
    amplitude = pl.pallas_call(
        amplitude_kernel,
        in_specs=vmem(2),
        out_specs=vmem(1)[0],
        out_shape=laid,
        scratch_shapes=[pltpu.VMEM((groups, virtual, LANES), F32)],
        compiler_params=ROOM,
        name="amplitude",
    )(direct, mirrored)

    kept = local // 2 * ROWS
    chunks = max(y_count // 2, 1)
    where = jnp.stack([y * local, zh])

    def contraction(swapped, dtype):
        return pl.pallas_call(
            functools.partial(contraction_kernel, orbitals=orbitals, swapped=swapped),
            in_specs=SMEM + vmem(1) + hbm(1),
            out_specs=vmem(1)[0],
            out_shape=jax.ShapeDtypeStruct((kept, virtual), dtype),
            scratch_shapes=[pltpu.VMEM((y_count, 2 * half, lanes), BF16), pltpu.SemaphoreType.DMA((chunks,))],
            compiler_params=BIG,
            cost_estimate=pl.CostEstimate(flops=kept * virtual * block * y_count * 4, bytes_accessed=y_count * 4 * half * lanes, transcendentals=0),
            name="contraction_sent" if swapped else "contraction_kept",
        )(where, amplitude, factors)

    received = lax.ppermute(contraction(True, BF16), "zh", [(0, 1), (1, 0)])
    return pl.pallas_call(
        finish_kernel,
        in_specs=vmem(2),
        out_specs=vmem(1)[0],
        out_shape=jax.ShapeDtypeStruct((local // 2, ROWS, virtual), BF16),
        compiler_params=SMALL,
        name="finish",
    )(contraction(False, F32), received)


def solution(mesh):
    rows, columns = mesh.devices.shape
    fine = Mesh(mesh.devices.reshape(rows // 2, 2, columns // 2, 2), ("p", "c", "y", "zh"))
    row, col = ("p", "c"), ("y", "zh")
    placed = (P(None, row, col), P(col, None), P(col, None), P(col, None))
    return jax.shard_map(body, mesh=fine, in_specs=placed, out_specs=P(col, row, None), check_vma=False)
```

```python
import functools

import jax
import jax.numpy as jnp
from jax import lax
from jax.experimental import pallas as pl
from jax.experimental.pallas import tpu as pltpu
from jax.sharding import Mesh, PartitionSpec as P

ROWS, SLOT, LANES, FOLD = 25, 32, 128, 13
F32, BF16 = jnp.float32, jnp.bfloat16


def pack_kernel(core_ref, first_hbm, weights_hbm, second_hbm, out_ref, held, sems):
    virtual, block = first_hbm.shape
    half = weights_hbm.shape[0] // 2
    out_ref[:, LANES:] = jnp.zeros((out_ref.shape[0], out_ref.shape[1] - LANES), BF16)

    def fetch(big_hbm, big_at, small_from, small_at):
        big = pltpu.make_async_copy(big_hbm, held.at[pl.ds(big_at, virtual)], sems.at[0])
        small = pltpu.make_async_copy(weights_hbm.at[pl.ds(small_from, half)], held.at[pl.ds(small_at, half)], sems.at[1])
        big.start()
        small.start()
        big.wait()
        small.wait()

    @pl.when(core_ref[0] == 0)
    def _():
        fetch(first_hbm, 0, 0, virtual)

    @pl.when(core_ref[0] != 0)
    def _():
        fetch(second_hbm, half, half, 0)

    out_ref[:, :block] = held[...]


def unfold(whole):
    front, back = FOLD, ROWS - FOLD
    tail = jnp.concatenate([whole[ROWS : ROWS + front], pltpu.roll(whole[ROWS : ROWS + front], LANES // 2, 1)[:back]], 0)
    return [whole[:ROWS], tail]


def direct_kernel(pieces_ref, out_ref, wide_ref, pick_ref):
    count = pieces_ref.shape[0]
    orbitals = out_ref.shape[0] // SLOT
    depth, width = pick_ref.shape
    at = lax.broadcasted_iota(jnp.int32, (depth, width), 0)
    to = lax.broadcasted_iota(jnp.int32, (depth, width), 1)
    within = at % SLOT
    target = jnp.where(within < ROWS, (at // SLOT) * ROWS + within, -1)
    pick_ref[...] = jnp.where(target == to, 1.0, 0.0).astype(BF16)
    lane = lax.broadcasted_iota(jnp.int32, (ROWS, LANES), 1) // SLOT
    wide_ref[...] = jnp.zeros_like(wide_ref)
    for quad in range(count // 4):
        parts = [unfold(pieces_ref[4 * quad + k].astype(F32)) for k in range(4)]
        for orbital in range(orbitals):
            placed = None
            for k in range(4):
                shift = SLOT * ((k - orbital) % 4)
                part = parts[k][orbital // 4]
                moved = pltpu.roll(part, shift, 1) if shift else part
                placed = moved if placed is None else jnp.where(lane == k, moved, placed)
            wide_ref[orbital * SLOT : orbital * SLOT + ROWS, quad * LANES : (quad + 1) * LANES] = placed
    out_ref[...] = jnp.dot(wide_ref[...].astype(BF16), pick_ref[...], preferred_element_type=F32).astype(BF16)


def amplitude_kernel(direct_ref, pieces_ref, out_ref, flat_ref):
    count = pieces_ref.shape[0]
    orbitals = out_ref.shape[0] // ROWS
    for source in range(count):
        for group, part in enumerate(unfold(pieces_ref[source].astype(F32))):
            flat_ref[group, source * ROWS : (source + 1) * ROWS, :] = part
    rows = []
    for group in range(flat_ref.shape[0]):
        mirrored = jnp.transpose(flat_ref[group])
        for k in range(min(4, orbitals - 4 * group)):
            start = (4 * group + k) * SLOT
            rows.append(direct_ref[start : start + SLOT, :].astype(F32)[:ROWS] - mirrored[k * SLOT : k * SLOT + ROWS])
    out_ref[...] = jnp.concatenate(rows, 0).astype(BF16)


def contraction_kernel(first_ref, amplitude_ref, factors_hbm, out_ref, held, sems, *, orbitals):
    rows, depth = amplitude_ref.shape
    chunks = sems.shape[0]
    per = factors_hbm.shape[0] // chunks
    copies = [
        pltpu.make_async_copy(factors_hbm.at[pl.ds(j * per, per)], held.at[pl.ds(j * per, per)], sems.at[j])
        for j in range(chunks)
    ]
    for copy in copies:
        copy.start()
    begin = (lax.broadcasted_iota(jnp.int32, (rows, orbitals), 1) - first_ref[0]) * ROWS
    row = lax.broadcasted_iota(jnp.int32, (rows, orbitals), 0)
    pick = jnp.where((row >= begin) & (row < begin + ROWS), 1.0, 0.0).astype(BF16)
    amplitude = amplitude_ref[...]
    total = None
    for j in range(chunks):
        copies[j].wait()
        scaled, second = [], []
        for k in range(j * per, (j + 1) * per):
            value = jnp.dot(amplitude, held[k, :depth], preferred_element_type=F32)
            scale = jnp.dot(pick, held[k, depth : depth + orbitals], preferred_element_type=F32)
            scaled.append((value * scale).astype(BF16))
            second.append(held[k, depth + orbitals : 2 * depth + orbitals])
        part = lax.dot_general(
            jnp.concatenate(scaled, 1), jnp.concatenate(second, 1), (((1,), (1,)), ((), ())), preferred_element_type=F32
        )
        total = part if total is None else total + part
    out_ref[...] = total.astype(out_ref.dtype)


def finish_kernel(own_ref, received_ref, out_ref):
    received = received_ref[...].astype(F32)
    for k in range(out_ref.shape[0]):
        rows = slice(k * ROWS, (k + 1) * ROWS)
        out_ref[k] = (own_ref[rows] + received[rows]).astype(BF16)


def vmem(count):
    return [pl.BlockSpec(memory_space=pltpu.VMEM)] * count


def hbm(count):
    return [pl.BlockSpec(memory_space=pltpu.HBM)] * count


SMEM = [pl.BlockSpec(memory_space=pltpu.SMEM)]
ROOM = pltpu.CompilerParams(vmem_limit_bytes=32 * 2**20)
SMALL = pltpu.CompilerParams(vmem_limit_bytes=16 * 2**20)
BIG = pltpu.CompilerParams(vmem_limit_bytes=48 * 2**20)
FULL = pltpu.CompilerParams(vmem_limit_bytes=60 * 2**20)


def body(halves, first_factor, second_factor, weights):
    y_count, row_count = lax.axis_size("y"), lax.axis_size("p") * 2
    orbitals = halves.shape[0]
    block, virtual = first_factor.shape
    columns = 2 * y_count
    local = orbitals // columns
    column, core = lax.axis_index(("y", "zh")), lax.axis_index("c")

    lanes = (block + LANES - 1) // LANES * LANES
    half = virtual + orbitals // 2
    share = pl.pallas_call(
        pack_kernel,
        in_specs=SMEM + hbm(3),
        out_specs=vmem(1)[0],
        out_shape=jax.ShapeDtypeStruct((half, lanes), BF16),
        scratch_shapes=[pltpu.VMEM((half, block), BF16), pltpu.SemaphoreType.DMA((2,))],
        compiler_params=FULL,
        name="pack",
    )(core.reshape(1), first_factor.T, weights.T, second_factor.T)
    factors = lax.all_gather(share, ("y", "c"), axis=0, tiled=True).reshape(y_count, 2 * half, lanes)

    height = (ROWS + FOLD + 7) // 8 * 8
    split = halves.reshape(columns, local, ROWS, 2, ROWS).transpose(0, 3, 2, 1, 4)
    split = jnp.pad(split, ((0, 0),) * 4 + ((0, SLOT - ROWS),))
    four = split[:, :, :, :4].reshape(columns, 2, ROWS, LANES)
    two = split[:, :, :, 4:].reshape(columns, 2, ROWS, LANES // 2)
    fold = jnp.pad(two[:, :, FOLD:], ((0, 0), (0, 0), (0, 2 * FOLD - ROWS), (0, 0)))
    two = jnp.concatenate([two[:, :, :FOLD], fold], 3)
    spare = jnp.zeros((columns, 2, height - ROWS - FOLD, LANES), BF16)
    pieces = jnp.concatenate([four, two, spare], 2)
    direct = lax.all_to_all(pieces, ("y", "zh"), 0, 0, tiled=True).reshape(row_count, height, LANES)
    mirrored = lax.all_to_all(direct, ("p", "c"), 0, 0, tiled=True)
    slots, rows = local * SLOT, local * ROWS
    direct = pl.pallas_call(
        direct_kernel,
        in_specs=vmem(1),
        out_specs=vmem(1)[0],
        out_shape=jax.ShapeDtypeStruct((slots, virtual), BF16),
        scratch_shapes=[pltpu.VMEM((slots, row_count * SLOT), F32), pltpu.VMEM((row_count * SLOT, virtual), BF16)],
        compiler_params=ROOM,
        cost_estimate=pl.CostEstimate(flops=2 * slots * row_count * SLOT * virtual, bytes_accessed=4 * slots * virtual, transcendentals=0),
        name="direct",
    )(direct)
    amplitude = pl.pallas_call(
        amplitude_kernel,
        in_specs=vmem(2),
        out_specs=vmem(1)[0],
        out_shape=jax.ShapeDtypeStruct((rows, virtual), BF16),
        scratch_shapes=[pltpu.VMEM((2, virtual, LANES), F32)],
        compiler_params=ROOM,
        name="amplitude",
    )(direct, mirrored)

    chunks = max(y_count // 2, 1)

    def contraction(name, first, amplitude, dtype):
        return pl.pallas_call(
            functools.partial(contraction_kernel, orbitals=orbitals),
            in_specs=SMEM + vmem(1) + hbm(1),
            out_specs=vmem(1)[0],
            out_shape=jax.ShapeDtypeStruct((rows, virtual), dtype),
            scratch_shapes=[pltpu.VMEM((y_count, 2 * half, lanes), BF16), pltpu.SemaphoreType.DMA((chunks,))],
            compiler_params=BIG,
            cost_estimate=pl.CostEstimate(flops=rows * virtual * block * y_count * 4, bytes_accessed=y_count * 4 * half * lanes, transcendentals=0),
            name=name,
        )(first.reshape(1), amplitude, factors)

    swap = [(0, 1), (1, 0)]
    partner = column + 1 - 2 * lax.axis_index("zh")
    theirs = lax.ppermute(amplitude, "zh", swap)
    received = lax.ppermute(contraction("contraction_sent", partner * local, theirs, BF16), "zh", swap)
    kept = contraction("contraction_kept", column * local, amplitude, F32)
    return pl.pallas_call(
        finish_kernel,
        in_specs=vmem(2),
        out_specs=vmem(1)[0],
        out_shape=jax.ShapeDtypeStruct((local, ROWS, virtual), BF16),
        compiler_params=SMALL,
        name="finish",
    )(kept, received)


def solution(mesh):
    rows, columns = mesh.devices.shape
    fine = Mesh(mesh.devices.reshape(rows // 2, 2, columns // 2, 2), ("p", "c", "y", "zh"))
    row, col = ("p", "c"), ("y", "zh")
    placed = (P(None, row, col), P(col, None), P(col, None), P(col, None))
    return jax.shard_map(body, mesh=fine, in_specs=placed, out_specs=P(col, row, None), check_vma=False)
```

```python
import functools

import jax
import jax.numpy as jnp
from jax import lax
from jax.experimental import pallas as pl
from jax.experimental.pallas import tpu as pltpu
from jax.sharding import Mesh, PartitionSpec as P

ROWS, SLOT, LANES, FOLD = 25, 32, 128, 13
F32, BF16 = jnp.float32, jnp.bfloat16


def pack_kernel(core_ref, first_hbm, weights_hbm, second_hbm, out_ref, held, sems):
    virtual, block = first_hbm.shape
    half = weights_hbm.shape[0] // 2
    out_ref[:, LANES:] = jnp.zeros((out_ref.shape[0], out_ref.shape[1] - LANES), BF16)

    def fetch(big_hbm, big_at, small_from, small_at):
        big = pltpu.make_async_copy(big_hbm, held.at[pl.ds(big_at, virtual)], sems.at[0])
        small = pltpu.make_async_copy(weights_hbm.at[pl.ds(small_from, half)], held.at[pl.ds(small_at, half)], sems.at[1])
        big.start()
        small.start()
        big.wait()
        small.wait()

    @pl.when(core_ref[0] == 0)
    def _():
        fetch(first_hbm, 0, 0, virtual)

    @pl.when(core_ref[0] != 0)
    def _():
        fetch(second_hbm, half, half, 0)

    out_ref[:, :block] = held[...]


def unfold(whole):
    front, back = FOLD, ROWS - FOLD
    tail = jnp.concatenate([whole[ROWS : ROWS + front], pltpu.roll(whole[ROWS : ROWS + front], LANES // 2, 1)[:back]], 0)
    return [whole[:ROWS], tail]


def direct_kernel(pieces_ref, out_ref, wide_ref, pick_ref):
    count = pieces_ref.shape[0]
    orbitals = out_ref.shape[0] // ROWS
    depth, width = pick_ref.shape
    at = lax.broadcasted_iota(jnp.int32, (depth, width), 0)
    to = lax.broadcasted_iota(jnp.int32, (depth, width), 1)
    within = at % SLOT
    target = jnp.where(within < ROWS, (at // SLOT) * ROWS + within, -1)
    pick_ref[...] = jnp.where(target == to, 1.0, 0.0).astype(BF16)
    lane = lax.broadcasted_iota(jnp.int32, (ROWS, LANES), 1) // SLOT
    wide_ref[...] = jnp.zeros_like(wide_ref)
    for quad in range(count // 4):
        parts = [unfold(pieces_ref[4 * quad + k].astype(F32)) for k in range(4)]
        for orbital in range(orbitals):
            placed = None
            for k in range(4):
                shift = SLOT * ((k - orbital) % 4)
                part = parts[k][orbital // 4]
                moved = pltpu.roll(part, shift, 1) if shift else part
                placed = moved if placed is None else jnp.where(lane == k, moved, placed)
            wide_ref[orbital * SLOT : orbital * SLOT + ROWS, quad * LANES : (quad + 1) * LANES] = placed
    laid = jnp.dot(wide_ref[...].astype(BF16), pick_ref[...], preferred_element_type=F32)
    out_ref[...] = jnp.concatenate([laid[k * SLOT : k * SLOT + ROWS] for k in range(orbitals)], 0).astype(BF16)


def amplitude_kernel(side_ref, direct_ref, pieces_ref, out_ref, flat_ref):
    count = pieces_ref.shape[0]
    orbitals = out_ref.shape[0] // ROWS
    for source in range(count):
        for group, part in enumerate(unfold(pieces_ref[source, side_ref[0]].astype(F32))):
            flat_ref[group, source * ROWS : (source + 1) * ROWS, :] = part
    rows = []
    for group in range(flat_ref.shape[0]):
        mirrored = jnp.transpose(flat_ref[group])
        for k in range(min(4, orbitals - 4 * group)):
            rows.append(mirrored[k * SLOT : k * SLOT + ROWS])
    out_ref[...] = (direct_ref[...].astype(F32) - jnp.concatenate(rows, 0)).astype(BF16)


def contraction_kernel(first_ref, amplitude_ref, factors_hbm, out_ref, held, sems, *, orbitals):
    rows, depth = amplitude_ref.shape
    chunks = sems.shape[0]
    per = factors_hbm.shape[0] // chunks
    copies = [
        pltpu.make_async_copy(factors_hbm.at[pl.ds(j * per, per)], held.at[pl.ds(j * per, per)], sems.at[j])
        for j in range(chunks)
    ]
    for copy in copies:
        copy.start()
    begin = (lax.broadcasted_iota(jnp.int32, (rows, orbitals), 1) - first_ref[0]) * ROWS
    row = lax.broadcasted_iota(jnp.int32, (rows, orbitals), 0)
    pick = jnp.where((row >= begin) & (row < begin + ROWS), 1.0, 0.0).astype(BF16)
    amplitude = amplitude_ref[...]
    total = None
    for j in range(chunks):
        copies[j].wait()
        scaled, second = [], []
        for k in range(j * per, (j + 1) * per):
            value = jnp.dot(amplitude, held[k, :depth], preferred_element_type=F32)
            scale = jnp.dot(pick, held[k, depth : depth + orbitals], preferred_element_type=F32)
            scaled.append((value * scale).astype(BF16))
            second.append(held[k, depth + orbitals : 2 * depth + orbitals])
        part = lax.dot_general(
            jnp.concatenate(scaled, 1), jnp.concatenate(second, 1), (((1,), (1,)), ((), ())), preferred_element_type=F32
        )
        total = part if total is None else total + part
    out_ref[...] = total.astype(out_ref.dtype)


def finish_kernel(own_ref, received_ref, out_ref):
    received = received_ref[...].astype(F32)
    for k in range(out_ref.shape[0]):
        rows = slice(k * ROWS, (k + 1) * ROWS)
        out_ref[k] = (own_ref[rows] + received[rows]).astype(BF16)


def vmem(count):
    return [pl.BlockSpec(memory_space=pltpu.VMEM)] * count


def hbm(count):
    return [pl.BlockSpec(memory_space=pltpu.HBM)] * count


SMEM = [pl.BlockSpec(memory_space=pltpu.SMEM)]
ROOM = pltpu.CompilerParams(vmem_limit_bytes=32 * 2**20)
SMALL = pltpu.CompilerParams(vmem_limit_bytes=16 * 2**20)
BIG = pltpu.CompilerParams(vmem_limit_bytes=48 * 2**20)
FULL = pltpu.CompilerParams(vmem_limit_bytes=60 * 2**20)


def body(halves, first_factor, second_factor, weights):
    y_count, row_count = lax.axis_size("y"), lax.axis_size("p") * 2
    orbitals = halves.shape[0]
    block, virtual = first_factor.shape
    columns = 2 * y_count
    local = orbitals // columns
    column, core = lax.axis_index(("y", "zh")), lax.axis_index("c")

    lanes = (block + LANES - 1) // LANES * LANES
    half = virtual + orbitals // 2
    share = pl.pallas_call(
        pack_kernel,
        in_specs=SMEM + hbm(3),
        out_specs=vmem(1)[0],
        out_shape=jax.ShapeDtypeStruct((half, lanes), BF16),
        scratch_shapes=[pltpu.VMEM((half, block), BF16), pltpu.SemaphoreType.DMA((2,))],
        compiler_params=FULL,
        name="pack",
    )(core.reshape(1), first_factor.T, weights.T, second_factor.T)
    factors = lax.all_gather(share, ("y", "c"), axis=0, tiled=True).reshape(y_count, 2 * half, lanes)

    height = (ROWS + FOLD + 7) // 8 * 8
    split = halves.reshape(columns, local, ROWS, 2, ROWS).transpose(0, 3, 2, 1, 4)
    split = jnp.pad(split, ((0, 0),) * 4 + ((0, SLOT - ROWS),))
    four = split[:, :, :, :4].reshape(columns, 2, ROWS, LANES)
    two = split[:, :, :, 4:].reshape(columns, 2, ROWS, LANES // 2)
    fold = jnp.pad(two[:, :, FOLD:], ((0, 0), (0, 0), (0, 2 * FOLD - ROWS), (0, 0)))
    two = jnp.concatenate([two[:, :, :FOLD], fold], 3)
    spare = jnp.zeros((columns, 2, height - ROWS - FOLD, LANES), BF16)
    pieces = jnp.concatenate([four, two, spare], 2)
    direct = lax.all_to_all(pieces, ("y", "zh"), 0, 0, tiled=True).reshape(row_count, height, LANES)
    both = jnp.broadcast_to(direct[:, None], (row_count, 2, height, LANES)).reshape(2 * row_count, height, LANES)
    mirrored = lax.all_to_all(both, ("p", "c", "zh"), 0, 0, tiled=True).reshape(row_count, 2, height, LANES)
    slots, rows = local * SLOT, local * ROWS
    laid = jax.ShapeDtypeStruct((rows, virtual), BF16)
    direct = pl.pallas_call(
        direct_kernel,
        in_specs=vmem(1),
        out_specs=vmem(1)[0],
        out_shape=laid,
        scratch_shapes=[pltpu.VMEM((slots, row_count * SLOT), F32), pltpu.VMEM((row_count * SLOT, virtual), BF16)],
        compiler_params=ROOM,
        cost_estimate=pl.CostEstimate(flops=2 * slots * row_count * SLOT * virtual, bytes_accessed=4 * slots * virtual, transcendentals=0),
        name="direct",
    )(direct)

    def amplitude(name, side, direct):
        return pl.pallas_call(
            amplitude_kernel,
            in_specs=SMEM + vmem(2),
            out_specs=vmem(1)[0],
            out_shape=laid,
            scratch_shapes=[pltpu.VMEM((2, virtual, LANES), F32)],
            compiler_params=ROOM,
            name=name,
        )(side.reshape(1), direct, mirrored)

    chunks = max(y_count // 2, 1)

    def contraction(name, first, amplitude, dtype):
        return pl.pallas_call(
            functools.partial(contraction_kernel, orbitals=orbitals),
            in_specs=SMEM + vmem(1) + hbm(1),
            out_specs=vmem(1)[0],
            out_shape=jax.ShapeDtypeStruct((rows, virtual), dtype),
            scratch_shapes=[pltpu.VMEM((y_count, 2 * half, lanes), BF16), pltpu.SemaphoreType.DMA((chunks,))],
            compiler_params=BIG,
            cost_estimate=pl.CostEstimate(flops=rows * virtual * block * y_count * 4, bytes_accessed=y_count * 4 * half * lanes, transcendentals=0),
            name=name,
        )(first.reshape(1), amplitude, factors)

    swap = [(0, 1), (1, 0)]
    side = lax.axis_index("zh")
    partner = column + 1 - 2 * side
    theirs = amplitude("amplitude_sent", 1 - side, lax.ppermute(direct, "zh", swap))
    received = lax.ppermute(contraction("contraction_sent", partner * local, theirs, BF16), "zh", swap)
    ours = amplitude("amplitude_kept", side, direct)
    kept = contraction("contraction_kept", column * local, ours, F32)
    return pl.pallas_call(
        finish_kernel,
        in_specs=vmem(2),
        out_specs=vmem(1)[0],
        out_shape=jax.ShapeDtypeStruct((local, ROWS, virtual), BF16),
        compiler_params=SMALL,
        name="finish",
    )(kept, received)


def solution(mesh):
    rows, columns = mesh.devices.shape
    fine = Mesh(mesh.devices.reshape(rows // 2, 2, columns // 2, 2), ("p", "c", "y", "zh"))
    row, col = ("p", "c"), ("y", "zh")
    placed = (P(None, row, col), P(col, None), P(col, None), P(col, None))
    return jax.shard_map(body, mesh=fine, in_specs=placed, out_specs=P(col, row, None), check_vma=False)
```

```python
import functools

import jax
import jax.numpy as jnp
from jax import lax
from jax.experimental import pallas as pl
from jax.experimental.pallas import tpu as pltpu
from jax.sharding import Mesh, PartitionSpec as P

ROWS, SLOT, LANES, FOLD = 25, 32, 128, 13
F32, BF16 = jnp.float32, jnp.bfloat16


def pack_kernel(core_ref, first_hbm, weights_hbm, second_hbm, out_ref, held, sems):
    virtual, block = first_hbm.shape
    half = weights_hbm.shape[0] // 2
    out_ref[:, LANES:] = jnp.zeros((out_ref.shape[0], out_ref.shape[1] - LANES), BF16)

    def fetch(big_hbm, big_at, small_from, small_at):
        big = pltpu.make_async_copy(big_hbm, held.at[pl.ds(big_at, virtual)], sems.at[0])
        small = pltpu.make_async_copy(weights_hbm.at[pl.ds(small_from, half)], held.at[pl.ds(small_at, half)], sems.at[1])
        big.start()
        small.start()
        big.wait()
        small.wait()

    @pl.when(core_ref[0] == 0)
    def _():
        fetch(first_hbm, 0, 0, virtual)

    @pl.when(core_ref[0] != 0)
    def _():
        fetch(second_hbm, half, half, 0)

    out_ref[:, :block] = held[...]


def unfold(whole):
    front, back = FOLD, ROWS - FOLD
    tail = jnp.concatenate([whole[ROWS : ROWS + front], pltpu.roll(whole[ROWS : ROWS + front], LANES // 2, 1)[:back]], 0)
    return [whole[:ROWS], tail]


def direct_kernel(pieces_ref, out_ref, wide_ref, pick_ref):
    count = pieces_ref.shape[0]
    orbitals = out_ref.shape[0] // SLOT
    depth, width = pick_ref.shape
    at = lax.broadcasted_iota(jnp.int32, (depth, width), 0)
    to = lax.broadcasted_iota(jnp.int32, (depth, width), 1)
    within = at % SLOT
    target = jnp.where(within < ROWS, (at // SLOT) * ROWS + within, -1)
    pick_ref[...] = jnp.where(target == to, 1.0, 0.0).astype(BF16)
    lane = lax.broadcasted_iota(jnp.int32, (ROWS, LANES), 1) // SLOT
    wide_ref[...] = jnp.zeros_like(wide_ref)
    for quad in range(count // 4):
        parts = [unfold(pieces_ref[4 * quad + k].astype(F32)) for k in range(4)]
        for orbital in range(orbitals):
            placed = None
            for k in range(4):
                shift = SLOT * ((k - orbital) % 4)
                part = parts[k][orbital // 4]
                moved = pltpu.roll(part, shift, 1) if shift else part
                placed = moved if placed is None else jnp.where(lane == k, moved, placed)
            wide_ref[orbital * SLOT : orbital * SLOT + ROWS, quad * LANES : (quad + 1) * LANES] = placed
    out_ref[...] = jnp.dot(wide_ref[...].astype(BF16), pick_ref[...], preferred_element_type=F32).astype(BF16)


def packed_height(rows, width):
    full, tail = divmod(width, LANES)
    stride = -(-rows // 8) * 8
    per = LANES // tail if tail else 1
    deep = -(-rows // per) if tail else 0
    return full, tail, stride, per, deep, full * stride + -(-deep // 8) * 8


def store_packed(out_ref, value):
    rows, width = value.shape
    full, tail, stride, per, deep, _ = packed_height(rows, width)
    for j in range(full):
        out_ref[j * stride : j * stride + rows, :] = value[:, j * LANES : (j + 1) * LANES].astype(out_ref.dtype)
    if tail:
        rest = value[:, full * LANES :]
        if per * deep > rows:
            rest = jnp.concatenate([rest, jnp.zeros((per * deep - rows, tail), F32)], 0)
        rest = jnp.concatenate([rest[k * deep : (k + 1) * deep] for k in range(per)], 1)
        out_ref[full * stride : full * stride + deep, : per * tail] = rest.astype(out_ref.dtype)


def load_packed(ref, rows, width):
    full, tail, stride, per, deep, _ = packed_height(rows, width)
    parts = [ref[j * stride : j * stride + rows, :].astype(F32) for j in range(full)]
    if tail:
        rest = ref[full * stride : full * stride + deep, :].astype(F32)
        parts.append(jnp.concatenate([rest[:, k * tail : (k + 1) * tail] for k in range(per)], 0)[:rows])
    return jnp.concatenate(parts, 1)


def amplitude_kernel(direct_ref, pieces_ref, out_ref, packed_ref, flat_ref):
    count = pieces_ref.shape[0]
    orbitals = out_ref.shape[0] // ROWS
    for source in range(count):
        for group, part in enumerate(unfold(pieces_ref[source].astype(F32))):
            flat_ref[group, source * ROWS : (source + 1) * ROWS, :] = part
    rows = []
    for group in range(flat_ref.shape[0]):
        mirrored = jnp.transpose(flat_ref[group])
        for k in range(min(4, orbitals - 4 * group)):
            start = (4 * group + k) * SLOT
            rows.append(direct_ref[start : start + SLOT, :].astype(F32)[:ROWS] - mirrored[k * SLOT : k * SLOT + ROWS])
    value = jnp.concatenate(rows, 0)
    out_ref[...] = value.astype(BF16)
    store_packed(packed_ref, value)


def contraction_kernel(first_ref, amplitude_ref, factors_hbm, out_ref, held, sems, *, orbitals, rows, depth, packed):
    chunks = sems.shape[0]
    per = factors_hbm.shape[0] // chunks
    copies = [
        pltpu.make_async_copy(factors_hbm.at[pl.ds(j * per, per)], held.at[pl.ds(j * per, per)], sems.at[j])
        for j in range(chunks)
    ]
    for copy in copies:
        copy.start()
    begin = (lax.broadcasted_iota(jnp.int32, (rows, orbitals), 1) - first_ref[0]) * ROWS
    row = lax.broadcasted_iota(jnp.int32, (rows, orbitals), 0)
    pick = jnp.where((row >= begin) & (row < begin + ROWS), 1.0, 0.0).astype(BF16)
    amplitude = load_packed(amplitude_ref, rows, depth).astype(BF16) if packed else amplitude_ref[...]
    total = None
    for j in range(chunks):
        copies[j].wait()
        scaled, second = [], []
        for k in range(j * per, (j + 1) * per):
            value = jnp.dot(amplitude, held[k, :depth], preferred_element_type=F32)
            scale = jnp.dot(pick, held[k, depth : depth + orbitals], preferred_element_type=F32)
            scaled.append((value * scale).astype(BF16))
            second.append(held[k, depth + orbitals : 2 * depth + orbitals])
        part = lax.dot_general(
            jnp.concatenate(scaled, 1), jnp.concatenate(second, 1), (((1,), (1,)), ((), ())), preferred_element_type=F32
        )
        total = part if total is None else total + part
    if packed:
        store_packed(out_ref, total)
    else:
        out_ref[...] = total


def finish_kernel(own_ref, received_ref, out_ref):
    total = own_ref[...] + load_packed(received_ref, *own_ref.shape)
    for k in range(out_ref.shape[0]):
        out_ref[k] = total[k * ROWS : (k + 1) * ROWS].astype(BF16)


def vmem(count):
    return [pl.BlockSpec(memory_space=pltpu.VMEM)] * count


def hbm(count):
    return [pl.BlockSpec(memory_space=pltpu.HBM)] * count


SMEM = [pl.BlockSpec(memory_space=pltpu.SMEM)]
ROOM = pltpu.CompilerParams(vmem_limit_bytes=32 * 2**20)
SMALL = pltpu.CompilerParams(vmem_limit_bytes=16 * 2**20)
BIG = pltpu.CompilerParams(vmem_limit_bytes=48 * 2**20)
FULL = pltpu.CompilerParams(vmem_limit_bytes=60 * 2**20)


def body(halves, first_factor, second_factor, weights):
    y_count, row_count = lax.axis_size("y"), lax.axis_size("p") * 2
    orbitals = halves.shape[0]
    block, virtual = first_factor.shape
    columns = 2 * y_count
    local = orbitals // columns
    column, core = lax.axis_index(("y", "zh")), lax.axis_index("c")

    lanes = (block + LANES - 1) // LANES * LANES
    half = virtual + orbitals // 2
    share = pl.pallas_call(
        pack_kernel,
        in_specs=SMEM + hbm(3),
        out_specs=vmem(1)[0],
        out_shape=jax.ShapeDtypeStruct((half, lanes), BF16),
        scratch_shapes=[pltpu.VMEM((half, block), BF16), pltpu.SemaphoreType.DMA((2,))],
        compiler_params=FULL,
        name="pack",
    )(core.reshape(1), first_factor.T, weights.T, second_factor.T)
    factors = lax.all_gather(share, ("y", "c"), axis=0, tiled=True).reshape(y_count, 2 * half, lanes)

    height = (ROWS + FOLD + 7) // 8 * 8
    split = halves.reshape(columns, local, ROWS, 2, ROWS).transpose(0, 3, 2, 1, 4)
    split = jnp.pad(split, ((0, 0),) * 4 + ((0, SLOT - ROWS),))
    four = split[:, :, :, :4].reshape(columns, 2, ROWS, LANES)
    two = split[:, :, :, 4:].reshape(columns, 2, ROWS, LANES // 2)
    fold = jnp.pad(two[:, :, FOLD:], ((0, 0), (0, 0), (0, 2 * FOLD - ROWS), (0, 0)))
    two = jnp.concatenate([two[:, :, :FOLD], fold], 3)
    spare = jnp.zeros((columns, 2, height - ROWS - FOLD, LANES), BF16)
    pieces = jnp.concatenate([four, two, spare], 2)
    direct = lax.all_to_all(pieces, ("y", "zh"), 0, 0, tiled=True).reshape(row_count, height, LANES)
    mirrored = lax.all_to_all(direct, ("p", "c"), 0, 0, tiled=True)
    slots, rows = local * SLOT, local * ROWS
    direct = pl.pallas_call(
        direct_kernel,
        in_specs=vmem(1),
        out_specs=vmem(1)[0],
        out_shape=jax.ShapeDtypeStruct((slots, virtual), BF16),
        scratch_shapes=[pltpu.VMEM((slots, row_count * SLOT), F32), pltpu.VMEM((row_count * SLOT, virtual), BF16)],
        compiler_params=ROOM,
        cost_estimate=pl.CostEstimate(flops=2 * slots * row_count * SLOT * virtual, bytes_accessed=4 * slots * virtual, transcendentals=0),
        name="direct",
    )(direct)
    packed = jax.ShapeDtypeStruct((packed_height(rows, virtual)[-1], LANES), BF16)
    ours, amplitude = pl.pallas_call(
        amplitude_kernel,
        in_specs=vmem(2),
        out_specs=vmem(2),
        out_shape=[jax.ShapeDtypeStruct((rows, virtual), BF16), packed],
        scratch_shapes=[pltpu.VMEM((2, virtual, LANES), F32)],
        compiler_params=ROOM,
        name="amplitude",
    )(direct, mirrored)

    chunks = max(y_count // 2, 1)

    def contraction(name, first, amplitude, result):
        return pl.pallas_call(
            functools.partial(contraction_kernel, orbitals=orbitals, rows=rows, depth=virtual, packed=result is packed),
            in_specs=SMEM + vmem(1) + hbm(1),
            out_specs=vmem(1)[0],
            out_shape=result,
            scratch_shapes=[pltpu.VMEM((y_count, 2 * half, lanes), BF16), pltpu.SemaphoreType.DMA((chunks,))],
            compiler_params=BIG,
            cost_estimate=pl.CostEstimate(flops=rows * virtual * block * y_count * 4, bytes_accessed=y_count * 4 * half * lanes, transcendentals=0),
            name=name,
        )(first.reshape(1), amplitude, factors)

    swap = [(0, 1), (1, 0)]
    partner = column + 1 - 2 * lax.axis_index("zh")
    theirs = lax.ppermute(amplitude, "zh", swap)
    received = lax.ppermute(contraction("contraction_sent", partner * local, theirs, packed), "zh", swap)
    kept = contraction("contraction_kept", column * local, ours, jax.ShapeDtypeStruct((rows, virtual), F32))
    return pl.pallas_call(
        finish_kernel,
        in_specs=vmem(2),
        out_specs=vmem(1)[0],
        out_shape=jax.ShapeDtypeStruct((local, ROWS, virtual), BF16),
        compiler_params=SMALL,
        name="finish",
    )(kept, received)


def solution(mesh):
    rows, columns = mesh.devices.shape
    fine = Mesh(mesh.devices.reshape(rows // 2, 2, columns // 2, 2), ("p", "c", "y", "zh"))
    row, col = ("p", "c"), ("y", "zh")
    placed = (P(None, row, col), P(col, None), P(col, None), P(col, None))
    return jax.shard_map(body, mesh=fine, in_specs=placed, out_specs=P(col, row, None), check_vma=False)
```

```python
import functools

import jax
import jax.numpy as jnp
from jax import lax
from jax.experimental import pallas as pl
from jax.experimental.pallas import tpu as pltpu
from jax.sharding import Mesh, PartitionSpec as P

ROWS, SLOT, LANES, FOLD = 25, 32, 128, 13
F32, BF16 = jnp.float32, jnp.bfloat16


def pack_kernel(core_ref, first_hbm, weights_hbm, second_hbm, out_ref, held, sems):
    virtual, block = first_hbm.shape
    half = weights_hbm.shape[0] // 2
    out_ref[:, LANES:] = jnp.zeros((out_ref.shape[0], out_ref.shape[1] - LANES), BF16)

    def fetch(big_hbm, big_at, small_from, small_at):
        big = pltpu.make_async_copy(big_hbm, held.at[pl.ds(big_at, virtual)], sems.at[0])
        small = pltpu.make_async_copy(weights_hbm.at[pl.ds(small_from, half)], held.at[pl.ds(small_at, half)], sems.at[1])
        big.start()
        small.start()
        big.wait()
        small.wait()

    @pl.when(core_ref[0] == 0)
    def _():
        fetch(first_hbm, 0, 0, virtual)

    @pl.when(core_ref[0] != 0)
    def _():
        fetch(second_hbm, half, half, 0)

    out_ref[:, :block] = held[...]


def unfold(whole):
    front, back = FOLD, ROWS - FOLD
    tail = jnp.concatenate([whole[ROWS : ROWS + front], pltpu.roll(whole[ROWS : ROWS + front], LANES // 2, 1)[:back]], 0)
    return [whole[:ROWS], tail]


def direct_kernel(pieces_ref, out_ref, wide_ref, pick_ref):
    count = pieces_ref.shape[0]
    orbitals = out_ref.shape[0] // SLOT
    depth, width = pick_ref.shape
    at = lax.broadcasted_iota(jnp.int32, (depth, width), 0)
    to = lax.broadcasted_iota(jnp.int32, (depth, width), 1)
    within = at % SLOT
    target = jnp.where(within < ROWS, (at // SLOT) * ROWS + within, -1)
    pick_ref[...] = jnp.where(target == to, 1.0, 0.0).astype(BF16)
    lane = lax.broadcasted_iota(jnp.int32, (ROWS, LANES), 1) // SLOT
    wide_ref[...] = jnp.zeros_like(wide_ref)
    for quad in range(count // 4):
        parts = [unfold(pieces_ref[4 * quad + k].astype(F32)) for k in range(4)]
        for orbital in range(orbitals):
            placed = None
            for k in range(4):
                shift = SLOT * ((k - orbital) % 4)
                part = parts[k][orbital // 4]
                moved = pltpu.roll(part, shift, 1) if shift else part
                placed = moved if placed is None else jnp.where(lane == k, moved, placed)
            wide_ref[orbital * SLOT : orbital * SLOT + ROWS, quad * LANES : (quad + 1) * LANES] = placed
    out_ref[...] = jnp.dot(wide_ref[...].astype(BF16), pick_ref[...], preferred_element_type=F32).astype(BF16)


def packed_height(rows, width):
    full, tail = divmod(width, LANES)
    stride = -(-rows // 8) * 8
    per = LANES // tail if tail else 1
    deep = -(-rows // per) if tail else 0
    return full, tail, stride, per, deep, full * stride + -(-deep // 8) * 8


def store_packed(out_ref, value):
    rows, width = value.shape
    full, tail, stride, per, deep, _ = packed_height(rows, width)
    for j in range(full):
        out_ref[j * stride : j * stride + rows, :] = value[:, j * LANES : (j + 1) * LANES].astype(out_ref.dtype)
    if tail:
        rest = value[:, full * LANES :]
        if per * deep > rows:
            rest = jnp.concatenate([rest, jnp.zeros((per * deep - rows, tail), F32)], 0)
        rest = jnp.concatenate([rest[k * deep : (k + 1) * deep] for k in range(per)], 1)
        out_ref[full * stride : full * stride + deep, : per * tail] = rest.astype(out_ref.dtype)


def load_packed(ref, rows, width):
    full, tail, stride, per, deep, _ = packed_height(rows, width)
    parts = [ref[j * stride : j * stride + rows, :].astype(F32) for j in range(full)]
    if tail:
        rest = ref[full * stride : full * stride + deep, :].astype(F32)
        parts.append(jnp.concatenate([rest[:, k * tail : (k + 1) * tail] for k in range(per)], 0)[:rows])
    return jnp.concatenate(parts, 1)


def amplitude_kernel(direct_ref, pieces_ref, out_ref, packed_ref, flat_ref):
    count = pieces_ref.shape[0]
    orbitals = out_ref.shape[0] // ROWS
    for source in range(count):
        for group, part in enumerate(unfold(pieces_ref[source].astype(F32))):
            flat_ref[group, source * ROWS : (source + 1) * ROWS, :] = part
    rows = []
    for group in range(flat_ref.shape[0]):
        mirrored = jnp.transpose(flat_ref[group])
        for k in range(min(4, orbitals - 4 * group)):
            start = (4 * group + k) * SLOT
            rows.append(direct_ref[start : start + SLOT, :].astype(F32)[:ROWS] - mirrored[k * SLOT : k * SLOT + ROWS])
    value = jnp.concatenate(rows, 0)
    out_ref[...] = value.astype(BF16)
    store_packed(packed_ref, value)


def ready_kernel(held, out_ref):
    out_ref[...] = held[0, :16, :LANES]


def contraction_kernel(first_ref, amplitude_ref, held, ready_ref, out_ref, *, orbitals, rows, depth, packed, chunks):
    per = held.shape[0] // chunks
    begin = (lax.broadcasted_iota(jnp.int32, (rows, orbitals), 1) - first_ref[0]) * ROWS
    row = lax.broadcasted_iota(jnp.int32, (rows, orbitals), 0)
    pick = jnp.where((row >= begin) & (row < begin + ROWS), 1.0, 0.0).astype(BF16)
    amplitude = load_packed(amplitude_ref, rows, depth).astype(BF16) if packed else amplitude_ref[...]
    total = None
    for j in range(chunks):
        scaled, second = [], []
        for k in range(j * per, (j + 1) * per):
            value = jnp.dot(amplitude, held[k, :depth], preferred_element_type=F32)
            scale = jnp.dot(pick, held[k, depth : depth + orbitals], preferred_element_type=F32)
            scaled.append((value * scale).astype(BF16))
            second.append(held[k, depth + orbitals : 2 * depth + orbitals])
        part = lax.dot_general(
            jnp.concatenate(scaled, 1), jnp.concatenate(second, 1), (((1,), (1,)), ((), ())), preferred_element_type=F32
        )
        total = part if total is None else total + part
    if packed:
        store_packed(out_ref, total)
    else:
        out_ref[...] = total


def finish_kernel(own_ref, received_ref, out_ref):
    total = own_ref[...] + load_packed(received_ref, *own_ref.shape)
    for k in range(out_ref.shape[0]):
        out_ref[k] = total[k * ROWS : (k + 1) * ROWS].astype(BF16)


def vmem(count):
    return [pl.BlockSpec(memory_space=pltpu.VMEM)] * count


def hbm(count):
    return [pl.BlockSpec(memory_space=pltpu.HBM)] * count


SMEM = [pl.BlockSpec(memory_space=pltpu.SMEM)]
ROOM = pltpu.CompilerParams(vmem_limit_bytes=32 * 2**20)
SMALL = pltpu.CompilerParams(vmem_limit_bytes=16 * 2**20)
BIG = pltpu.CompilerParams(vmem_limit_bytes=32 * 2**20)
FETCH = pltpu.CompilerParams(vmem_limit_bytes=32 * 2**20)
FULL = pltpu.CompilerParams(vmem_limit_bytes=60 * 2**20)


def body(halves, first_factor, second_factor, weights):
    y_count, row_count = lax.axis_size("y"), lax.axis_size("p") * 2
    orbitals = halves.shape[0]
    block, virtual = first_factor.shape
    columns = 2 * y_count
    local = orbitals // columns
    column, core = lax.axis_index(("y", "zh")), lax.axis_index("c")

    lanes = (block + LANES - 1) // LANES * LANES
    half = virtual + orbitals // 2
    share = pl.pallas_call(
        pack_kernel,
        in_specs=SMEM + hbm(3),
        out_specs=vmem(1)[0],
        out_shape=jax.ShapeDtypeStruct((half, lanes), BF16),
        scratch_shapes=[pltpu.VMEM((half, block), BF16), pltpu.SemaphoreType.DMA((2,))],
        compiler_params=FULL,
        name="pack",
    )(core.reshape(1), first_factor.T, weights.T, second_factor.T)
    factors = lax.all_gather(share, ("y", "c"), axis=0, tiled=True).reshape(y_count, 2 * half, lanes)

    height = (ROWS + FOLD + 7) // 8 * 8
    split = halves.reshape(columns, local, ROWS, 2, ROWS).transpose(0, 3, 2, 1, 4)
    split = jnp.pad(split, ((0, 0),) * 4 + ((0, SLOT - ROWS),))
    four = split[:, :, :, :4].reshape(columns, 2, ROWS, LANES)
    two = split[:, :, :, 4:].reshape(columns, 2, ROWS, LANES // 2)
    fold = jnp.pad(two[:, :, FOLD:], ((0, 0), (0, 0), (0, 2 * FOLD - ROWS), (0, 0)))
    two = jnp.concatenate([two[:, :, :FOLD], fold], 3)
    spare = jnp.zeros((columns, 2, height - ROWS - FOLD, LANES), BF16)
    pieces = jnp.concatenate([four, two, spare], 2)
    direct = lax.all_to_all(pieces, ("y", "zh"), 0, 0, tiled=True).reshape(row_count, height, LANES)
    mirrored = lax.all_to_all(direct, ("p", "c"), 0, 0, tiled=True)
    slots, rows = local * SLOT, local * ROWS
    direct = pl.pallas_call(
        direct_kernel,
        in_specs=vmem(1),
        out_specs=vmem(1)[0],
        out_shape=jax.ShapeDtypeStruct((slots, virtual), BF16),
        scratch_shapes=[pltpu.VMEM((slots, row_count * SLOT), F32), pltpu.VMEM((row_count * SLOT, virtual), BF16)],
        compiler_params=ROOM,
        cost_estimate=pl.CostEstimate(flops=2 * slots * row_count * SLOT * virtual, bytes_accessed=4 * slots * virtual, transcendentals=0),
        name="direct",
    )(direct)
    packed = jax.ShapeDtypeStruct((packed_height(rows, virtual)[-1], LANES), BF16)
    ours, amplitude = pl.pallas_call(
        amplitude_kernel,
        in_specs=vmem(2),
        out_specs=vmem(2),
        out_shape=[jax.ShapeDtypeStruct((rows, virtual), BF16), packed],
        scratch_shapes=[pltpu.VMEM((2, virtual, LANES), F32)],
        compiler_params=ROOM,
        name="amplitude",
    )(direct, mirrored)

    ready = pl.pallas_call(
        ready_kernel,
        in_specs=vmem(1),
        out_specs=vmem(1)[0],
        out_shape=jax.ShapeDtypeStruct((16, LANES), BF16),
        compiler_params=FETCH,
        cost_estimate=pl.CostEstimate(flops=0, bytes_accessed=2 * factors.size, transcendentals=0),
        name="ready",
    )(factors)

    def contraction(name, first, amplitude, result):
        return pl.pallas_call(
            functools.partial(
                contraction_kernel, orbitals=orbitals, rows=rows, depth=virtual, packed=result is packed, chunks=max(y_count // 2, 1)
            ),
            in_specs=SMEM + vmem(3),
            out_specs=vmem(1)[0],
            out_shape=result,
            compiler_params=BIG,
            cost_estimate=pl.CostEstimate(flops=rows * virtual * block * y_count * 4, bytes_accessed=y_count * 4 * half * lanes, transcendentals=0),
            name=name,
        )(first.reshape(1), amplitude, factors, ready)

    swap = [(0, 1), (1, 0)]
    partner = column + 1 - 2 * lax.axis_index("zh")
    theirs = lax.ppermute(amplitude, "zh", swap)
    received = lax.ppermute(contraction("contraction_sent", partner * local, theirs, packed), "zh", swap)
    kept = contraction("contraction_kept", column * local, ours, jax.ShapeDtypeStruct((rows, virtual), F32))
    return pl.pallas_call(
        finish_kernel,
        in_specs=vmem(2),
        out_specs=vmem(1)[0],
        out_shape=jax.ShapeDtypeStruct((local, ROWS, virtual), BF16),
        compiler_params=SMALL,
        name="finish",
    )(kept, received)


def solution(mesh):
    rows, columns = mesh.devices.shape
    fine = Mesh(mesh.devices.reshape(rows // 2, 2, columns // 2, 2), ("p", "c", "y", "zh"))
    row, col = ("p", "c"), ("y", "zh")
    placed = (P(None, row, col), P(col, None), P(col, None), P(col, None))
    return jax.shard_map(body, mesh=fine, in_specs=placed, out_specs=P(col, row, None), check_vma=False)
```

```python
import functools

import jax
import jax.numpy as jnp
from jax import lax
from jax.experimental import pallas as pl
from jax.experimental.pallas import tpu as pltpu
from jax.sharding import Mesh, PartitionSpec as P

ROWS, SLOT, LANES, FOLD = 25, 32, 128, 13
F32, BF16 = jnp.float32, jnp.bfloat16


def pack_kernel(core_ref, first_hbm, weights_hbm, second_hbm, out_ref, held, sems):
    virtual, block = first_hbm.shape
    half = weights_hbm.shape[0] // 2
    out_ref[:, LANES:] = jnp.zeros((out_ref.shape[0], out_ref.shape[1] - LANES), BF16)

    def fetch(big_hbm, big_at, small_from, small_at):
        big = pltpu.make_async_copy(big_hbm, held.at[pl.ds(big_at, virtual)], sems.at[0])
        small = pltpu.make_async_copy(weights_hbm.at[pl.ds(small_from, half)], held.at[pl.ds(small_at, half)], sems.at[1])
        big.start()
        small.start()
        big.wait()
        small.wait()

    @pl.when(core_ref[0] == 0)
    def _():
        fetch(first_hbm, 0, 0, virtual)

    @pl.when(core_ref[0] != 0)
    def _():
        fetch(second_hbm, half, half, 0)

    out_ref[:, :block] = held[...]


def unfold(whole):
    front, back = FOLD, ROWS - FOLD
    tail = jnp.concatenate([whole[ROWS : ROWS + front], pltpu.roll(whole[ROWS : ROWS + front], LANES // 2, 1)[:back]], 0)
    return [whole[:ROWS], tail]


def direct_kernel(pieces_ref, out_ref, wide_ref, pick_ref):
    count = pieces_ref.shape[0]
    orbitals = out_ref.shape[0] // SLOT
    depth, width = pick_ref.shape
    at = lax.broadcasted_iota(jnp.int32, (depth, width), 0)
    to = lax.broadcasted_iota(jnp.int32, (depth, width), 1)
    within = at % SLOT
    target = jnp.where(within < ROWS, (at // SLOT) * ROWS + within, -1)
    pick_ref[...] = jnp.where(target == to, 1.0, 0.0).astype(BF16)
    lane = lax.broadcasted_iota(jnp.int32, (ROWS, LANES), 1) // SLOT
    wide_ref[...] = jnp.zeros_like(wide_ref)
    for quad in range(count // 4):
        parts = [unfold(pieces_ref[4 * quad + k].astype(F32)) for k in range(4)]
        for orbital in range(orbitals):
            placed = None
            for k in range(4):
                shift = SLOT * ((k - orbital) % 4)
                part = parts[k][orbital // 4]
                moved = pltpu.roll(part, shift, 1) if shift else part
                placed = moved if placed is None else jnp.where(lane == k, moved, placed)
            wide_ref[orbital * SLOT : orbital * SLOT + ROWS, quad * LANES : (quad + 1) * LANES] = placed
    out_ref[...] = jnp.dot(wide_ref[...].astype(BF16), pick_ref[...], preferred_element_type=F32).astype(BF16)


def packed_height(rows, width):
    full, tail = divmod(width, LANES)
    stride = -(-rows // 8) * 8
    per = LANES // tail if tail else 1
    deep = -(-rows // per) if tail else 0
    return full, tail, stride, per, deep, full * stride + -(-deep // 8) * 8


def store_packed(out_ref, value):
    rows, width = value.shape
    full, tail, stride, per, deep, _ = packed_height(rows, width)
    for j in range(full):
        out_ref[j * stride : j * stride + rows, :] = value[:, j * LANES : (j + 1) * LANES].astype(out_ref.dtype)
    if tail:
        rest = value[:, full * LANES :]
        if per * deep > rows:
            rest = jnp.concatenate([rest, jnp.zeros((per * deep - rows, tail), F32)], 0)
        rest = jnp.concatenate([rest[k * deep : (k + 1) * deep] for k in range(per)], 1)
        out_ref[full * stride : full * stride + deep, : per * tail] = rest.astype(out_ref.dtype)


def load_packed(ref, rows, width):
    full, tail, stride, per, deep, _ = packed_height(rows, width)
    parts = [ref[j * stride : j * stride + rows, :].astype(F32) for j in range(full)]
    if tail:
        rest = ref[full * stride : full * stride + deep, :].astype(F32)
        parts.append(jnp.concatenate([rest[:, k * tail : (k + 1) * tail] for k in range(per)], 0)[:rows])
    return jnp.concatenate(parts, 1)


def amplitude_kernel(direct_ref, pieces_ref, out_ref, front_ref, back_ref, flat_ref):
    count = pieces_ref.shape[0]
    orbitals = out_ref.shape[0] // ROWS
    for source in range(count):
        for group, part in enumerate(unfold(pieces_ref[source].astype(F32))):
            flat_ref[group, source * ROWS : (source + 1) * ROWS, :] = part
    rows = []
    for group in range(flat_ref.shape[0]):
        mirrored = jnp.transpose(flat_ref[group])
        for k in range(min(4, orbitals - 4 * group)):
            start = (4 * group + k) * SLOT
            rows.append(direct_ref[start : start + SLOT, :].astype(F32)[:ROWS] - mirrored[k * SLOT : k * SLOT + ROWS])
    value = jnp.concatenate(rows, 0)
    out_ref[...] = value.astype(BF16)
    half = value.shape[0] // 2
    store_packed(front_ref, value[:half])
    store_packed(back_ref, value[half:])


def ready_kernel(held, out_ref):
    out_ref[...] = held[0, :16, :LANES]


def contraction_kernel(first_ref, amplitude_ref, held, ready_ref, out_ref, *, orbitals, rows, depth, packed, chunks):
    per = held.shape[0] // chunks
    begin = (lax.broadcasted_iota(jnp.int32, (rows, orbitals), 1) - first_ref[0]) * ROWS
    row = lax.broadcasted_iota(jnp.int32, (rows, orbitals), 0)
    pick = jnp.where((row >= begin) & (row < begin + ROWS), 1.0, 0.0).astype(BF16)
    amplitude = load_packed(amplitude_ref, rows, depth).astype(BF16) if packed else amplitude_ref[...]
    total = None
    for j in range(chunks):
        scaled, second = [], []
        for k in range(j * per, (j + 1) * per):
            value = jnp.dot(amplitude, held[k, :depth], preferred_element_type=F32)
            scale = jnp.dot(pick, held[k, depth : depth + orbitals], preferred_element_type=F32)
            scaled.append((value * scale).astype(BF16))
            second.append(held[k, depth + orbitals : 2 * depth + orbitals])
        part = lax.dot_general(
            jnp.concatenate(scaled, 1), jnp.concatenate(second, 1), (((1,), (1,)), ((), ())), preferred_element_type=F32
        )
        total = part if total is None else total + part
    if packed:
        store_packed(out_ref, total)
    else:
        out_ref[...] = total


def finish_kernel(own_ref, front_ref, back_ref, out_ref):
    rows, width = own_ref.shape
    received = [load_packed(ref, rows // 2, width) for ref in (front_ref, back_ref)]
    total = own_ref[...] + jnp.concatenate(received, 0)
    for k in range(out_ref.shape[0]):
        out_ref[k] = total[k * ROWS : (k + 1) * ROWS].astype(BF16)


def vmem(count):
    return [pl.BlockSpec(memory_space=pltpu.VMEM)] * count


def hbm(count):
    return [pl.BlockSpec(memory_space=pltpu.HBM)] * count


SMEM = [pl.BlockSpec(memory_space=pltpu.SMEM)]
ROOM = pltpu.CompilerParams(vmem_limit_bytes=32 * 2**20)
SMALL = pltpu.CompilerParams(vmem_limit_bytes=16 * 2**20)
BIG = pltpu.CompilerParams(vmem_limit_bytes=32 * 2**20)
FETCH = pltpu.CompilerParams(vmem_limit_bytes=32 * 2**20)
FULL = pltpu.CompilerParams(vmem_limit_bytes=60 * 2**20)


def body(halves, first_factor, second_factor, weights):
    y_count, row_count = lax.axis_size("y"), lax.axis_size("p") * 2
    orbitals = halves.shape[0]
    block, virtual = first_factor.shape
    columns = 2 * y_count
    local = orbitals // columns
    column, core = lax.axis_index(("y", "zh")), lax.axis_index("c")

    lanes = (block + LANES - 1) // LANES * LANES
    half = virtual + orbitals // 2
    share = pl.pallas_call(
        pack_kernel,
        in_specs=SMEM + hbm(3),
        out_specs=vmem(1)[0],
        out_shape=jax.ShapeDtypeStruct((half, lanes), BF16),
        scratch_shapes=[pltpu.VMEM((half, block), BF16), pltpu.SemaphoreType.DMA((2,))],
        compiler_params=FULL,
        name="pack",
    )(core.reshape(1), first_factor.T, weights.T, second_factor.T)
    factors = lax.all_gather(share, ("y", "c"), axis=0, tiled=True).reshape(y_count, 2 * half, lanes)

    height = (ROWS + FOLD + 7) // 8 * 8
    split = halves.reshape(columns, local, ROWS, 2, ROWS).transpose(0, 3, 2, 1, 4)
    split = jnp.pad(split, ((0, 0),) * 4 + ((0, SLOT - ROWS),))
    four = split[:, :, :, :4].reshape(columns, 2, ROWS, LANES)
    two = split[:, :, :, 4:].reshape(columns, 2, ROWS, LANES // 2)
    fold = jnp.pad(two[:, :, FOLD:], ((0, 0), (0, 0), (0, 2 * FOLD - ROWS), (0, 0)))
    two = jnp.concatenate([two[:, :, :FOLD], fold], 3)
    spare = jnp.zeros((columns, 2, height - ROWS - FOLD, LANES), BF16)
    pieces = jnp.concatenate([four, two, spare], 2)
    direct = lax.all_to_all(pieces, ("y", "zh"), 0, 0, tiled=True).reshape(row_count, height, LANES)
    mirrored = lax.all_to_all(direct, ("p", "c"), 0, 0, tiled=True)
    slots, rows = local * SLOT, local * ROWS
    direct = pl.pallas_call(
        direct_kernel,
        in_specs=vmem(1),
        out_specs=vmem(1)[0],
        out_shape=jax.ShapeDtypeStruct((slots, virtual), BF16),
        scratch_shapes=[pltpu.VMEM((slots, row_count * SLOT), F32), pltpu.VMEM((row_count * SLOT, virtual), BF16)],
        compiler_params=ROOM,
        cost_estimate=pl.CostEstimate(flops=2 * slots * row_count * SLOT * virtual, bytes_accessed=4 * slots * virtual, transcendentals=0),
        name="direct",
    )(direct)
    packed = jax.ShapeDtypeStruct((packed_height(rows // 2, virtual)[-1], LANES), BF16)
    ours, front, back = pl.pallas_call(
        amplitude_kernel,
        in_specs=vmem(2),
        out_specs=vmem(3),
        out_shape=[jax.ShapeDtypeStruct((rows, virtual), BF16), packed, packed],
        scratch_shapes=[pltpu.VMEM((2, virtual, LANES), F32)],
        compiler_params=ROOM,
        name="amplitude",
    )(direct, mirrored)

    ready = pl.pallas_call(
        ready_kernel,
        in_specs=vmem(1),
        out_specs=vmem(1)[0],
        out_shape=jax.ShapeDtypeStruct((16, LANES), BF16),
        compiler_params=FETCH,
        cost_estimate=pl.CostEstimate(flops=0, bytes_accessed=2 * factors.size, transcendentals=0),
        name="ready",
    )(factors)

    def contraction(name, first, amplitude, result):
        return pl.pallas_call(
            functools.partial(
                contraction_kernel, orbitals=orbitals, rows=rows // 2 if result is packed else rows, depth=virtual, packed=result is packed, chunks=max(y_count // 2, 1)
            ),
            in_specs=SMEM + vmem(3),
            out_specs=vmem(1)[0],
            out_shape=result,
            compiler_params=BIG,
            cost_estimate=pl.CostEstimate(flops=rows * virtual * block * y_count * 4, bytes_accessed=y_count * 4 * half * lanes, transcendentals=0),
            name=name,
        )(first.reshape(1), amplitude, factors, ready)

    swap = [(0, 1), (1, 0)]
    partner = column + 1 - 2 * lax.axis_index("zh")
    theirs = [lax.ppermute(part, "zh", swap) for part in (front, back)]
    received = [
        lax.ppermute(contraction(f"contraction_sent_{k}", partner * local + k * (local // 2), theirs[k], packed), "zh", swap)
        for k in range(2)
    ]
    kept = contraction("contraction_kept", column * local, ours, jax.ShapeDtypeStruct((rows, virtual), F32))
    return pl.pallas_call(
        finish_kernel,
        in_specs=vmem(3),
        out_specs=vmem(1)[0],
        out_shape=jax.ShapeDtypeStruct((local, ROWS, virtual), BF16),
        compiler_params=SMALL,
        name="finish",
    )(kept, *received)


def solution(mesh):
    rows, columns = mesh.devices.shape
    fine = Mesh(mesh.devices.reshape(rows // 2, 2, columns // 2, 2), ("p", "c", "y", "zh"))
    row, col = ("p", "c"), ("y", "zh")
    placed = (P(None, row, col), P(col, None), P(col, None), P(col, None))
    return jax.shard_map(body, mesh=fine, in_specs=placed, out_specs=P(col, row, None), check_vma=False)
```

```python
import functools

import jax
import jax.numpy as jnp
from jax import lax
from jax.experimental import pallas as pl
from jax.experimental.pallas import tpu as pltpu
from jax.sharding import Mesh, PartitionSpec as P

ROWS, SLOT, LANES, FOLD = 25, 32, 128, 13
F32, BF16 = jnp.float32, jnp.bfloat16


def pack_kernel(core_ref, first_hbm, weights_hbm, second_hbm, out_ref, held, sems):
    virtual, block = first_hbm.shape
    half = weights_hbm.shape[0] // 2
    out_ref[:, LANES:] = jnp.zeros((out_ref.shape[0], out_ref.shape[1] - LANES), BF16)

    def fetch(big_hbm, big_at, small_from, small_at):
        big = pltpu.make_async_copy(big_hbm, held.at[pl.ds(big_at, virtual)], sems.at[0])
        small = pltpu.make_async_copy(weights_hbm.at[pl.ds(small_from, half)], held.at[pl.ds(small_at, half)], sems.at[1])
        big.start()
        small.start()
        big.wait()
        small.wait()

    @pl.when(core_ref[0] == 0)
    def _():
        fetch(first_hbm, 0, 0, virtual)

    @pl.when(core_ref[0] != 0)
    def _():
        fetch(second_hbm, half, half, 0)

    out_ref[:, :block] = held[...]


def unfold(whole):
    front, back = FOLD, ROWS - FOLD
    tail = jnp.concatenate([whole[ROWS : ROWS + front], pltpu.roll(whole[ROWS : ROWS + front], LANES // 2, 1)[:back]], 0)
    return [whole[:ROWS], tail]


def direct_kernel(pieces_ref, out_ref, wide_ref, pick_ref):
    count = pieces_ref.shape[0]
    orbitals = out_ref.shape[0] // SLOT
    depth, width = pick_ref.shape
    at = lax.broadcasted_iota(jnp.int32, (depth, width), 0)
    to = lax.broadcasted_iota(jnp.int32, (depth, width), 1)
    within = at % SLOT
    target = jnp.where(within < ROWS, (at // SLOT) * ROWS + within, -1)
    pick_ref[...] = jnp.where(target == to, 1.0, 0.0).astype(BF16)
    lane = lax.broadcasted_iota(jnp.int32, (ROWS, LANES), 1) // SLOT
    wide_ref[...] = jnp.zeros_like(wide_ref)
    for quad in range(count // 4):
        parts = [unfold(pieces_ref[4 * quad + k].astype(F32)) for k in range(4)]
        for orbital in range(orbitals):
            placed = None
            for k in range(4):
                shift = SLOT * ((k - orbital) % 4)
                part = parts[k][orbital // 4]
                moved = pltpu.roll(part, shift, 1) if shift else part
                placed = moved if placed is None else jnp.where(lane == k, moved, placed)
            wide_ref[orbital * SLOT : orbital * SLOT + ROWS, quad * LANES : (quad + 1) * LANES] = placed
    out_ref[...] = jnp.dot(wide_ref[...].astype(BF16), pick_ref[...], preferred_element_type=F32).astype(BF16)


def packed_height(rows, width):
    full, tail = divmod(width, LANES)
    stride = -(-rows // 8) * 8
    per = LANES // tail if tail else 1
    deep = -(-rows // per) if tail else 0
    return full, tail, stride, per, deep, full * stride + -(-deep // 8) * 8


def store_packed(out_ref, value):
    rows, width = value.shape
    full, tail, stride, per, deep, _ = packed_height(rows, width)
    for j in range(full):
        out_ref[j * stride : j * stride + rows, :] = value[:, j * LANES : (j + 1) * LANES].astype(out_ref.dtype)
    if tail:
        rest = value[:, full * LANES :]
        if per * deep > rows:
            rest = jnp.concatenate([rest, jnp.zeros((per * deep - rows, tail), F32)], 0)
        rest = jnp.concatenate([rest[k * deep : (k + 1) * deep] for k in range(per)], 1)
        out_ref[full * stride : full * stride + deep, : per * tail] = rest.astype(out_ref.dtype)


def load_packed(ref, rows, width):
    full, tail, stride, per, deep, _ = packed_height(rows, width)
    parts = [ref[j * stride : j * stride + rows, :].astype(F32) for j in range(full)]
    if tail:
        rest = ref[full * stride : full * stride + deep, :].astype(F32)
        parts.append(jnp.concatenate([rest[:, k * tail : (k + 1) * tail] for k in range(per)], 0)[:rows])
    return jnp.concatenate(parts, 1)


def amplitude_kernel(direct_ref, pieces_ref, out_ref, front_ref, back_ref, flat_ref):
    count = pieces_ref.shape[0]
    orbitals = out_ref.shape[0] // ROWS
    for source in range(count):
        for group, part in enumerate(unfold(pieces_ref[source].astype(F32))):
            flat_ref[group, source * ROWS : (source + 1) * ROWS, :] = part
    rows = []
    for group in range(flat_ref.shape[0]):
        mirrored = jnp.transpose(flat_ref[group])
        for k in range(min(4, orbitals - 4 * group)):
            start = (4 * group + k) * SLOT
            rows.append(direct_ref[start : start + SLOT, :].astype(F32)[:ROWS] - mirrored[k * SLOT : k * SLOT + ROWS])
    value = jnp.concatenate(rows, 0)
    out_ref[...] = value.astype(BF16)
    half = value.shape[0] // 2
    store_packed(front_ref, value[:half])
    store_packed(back_ref, value[half:])


def ready_kernel(held, out_ref):
    out_ref[...] = held[0, :16, :LANES]


def contraction_kernel(first_ref, amplitude_ref, held, ready_ref, out_ref, *, orbitals, rows, depth, packed, chunks):
    per = held.shape[0] // chunks
    begin = (lax.broadcasted_iota(jnp.int32, (rows, orbitals), 1) - first_ref[0]) * ROWS
    row = lax.broadcasted_iota(jnp.int32, (rows, orbitals), 0)
    pick = jnp.where((row >= begin) & (row < begin + ROWS), 1.0, 0.0).astype(BF16)
    amplitude = load_packed(amplitude_ref, rows, depth).astype(BF16) if packed else amplitude_ref[...]
    total = None
    for j in range(chunks):
        scaled, second = [], []
        for k in range(j * per, (j + 1) * per):
            value = jnp.dot(amplitude, held[k, :depth], preferred_element_type=F32)
            scale = jnp.dot(pick, held[k, depth : depth + orbitals], preferred_element_type=F32)
            scaled.append((value * scale).astype(BF16))
            second.append(held[k, depth + orbitals : 2 * depth + orbitals])
        part = lax.dot_general(
            jnp.concatenate(scaled, 1), jnp.concatenate(second, 1), (((1,), (1,)), ((), ())), preferred_element_type=F32
        )
        total = part if total is None else total + part
    if packed:
        store_packed(out_ref, total)
    else:
        out_ref[...] = total


def streamed_kernel(first_ref, amplitude_ref, factors_hbm, out_ref, held, sems, *, orbitals, rows, depth, packed):
    chunks = sems.shape[0]
    per = factors_hbm.shape[0] // chunks
    copies = [
        pltpu.make_async_copy(factors_hbm.at[pl.ds(j * per, per)], held.at[pl.ds(j * per, per)], sems.at[j])
        for j in range(chunks)
    ]
    for copy in copies:
        copy.start()
    begin = (lax.broadcasted_iota(jnp.int32, (rows, orbitals), 1) - first_ref[0]) * ROWS
    row = lax.broadcasted_iota(jnp.int32, (rows, orbitals), 0)
    pick = jnp.where((row >= begin) & (row < begin + ROWS), 1.0, 0.0).astype(BF16)
    amplitude = load_packed(amplitude_ref, rows, depth).astype(BF16) if packed else amplitude_ref[...]
    total = None
    for j in range(chunks):
        copies[j].wait()
        scaled, second = [], []
        for k in range(j * per, (j + 1) * per):
            value = jnp.dot(amplitude, held[k, :depth], preferred_element_type=F32)
            scale = jnp.dot(pick, held[k, depth : depth + orbitals], preferred_element_type=F32)
            scaled.append((value * scale).astype(BF16))
            second.append(held[k, depth + orbitals : 2 * depth + orbitals])
        part = lax.dot_general(
            jnp.concatenate(scaled, 1), jnp.concatenate(second, 1), (((1,), (1,)), ((), ())), preferred_element_type=F32
        )
        total = part if total is None else total + part
    if packed:
        store_packed(out_ref, total)
    else:
        out_ref[...] = total


def finish_kernel(own_ref, front_ref, back_ref, out_ref):
    rows, width = own_ref.shape
    received = [load_packed(ref, rows // 2, width) for ref in (front_ref, back_ref)]
    total = own_ref[...] + jnp.concatenate(received, 0)
    for k in range(out_ref.shape[0]):
        out_ref[k] = total[k * ROWS : (k + 1) * ROWS].astype(BF16)


def vmem(count):
    return [pl.BlockSpec(memory_space=pltpu.VMEM)] * count


def hbm(count):
    return [pl.BlockSpec(memory_space=pltpu.HBM)] * count


SMEM = [pl.BlockSpec(memory_space=pltpu.SMEM)]
ROOM = pltpu.CompilerParams(vmem_limit_bytes=32 * 2**20)
SMALL = pltpu.CompilerParams(vmem_limit_bytes=16 * 2**20)
BIG = pltpu.CompilerParams(vmem_limit_bytes=32 * 2**20)
FETCH = pltpu.CompilerParams(vmem_limit_bytes=32 * 2**20)
FULL = pltpu.CompilerParams(vmem_limit_bytes=60 * 2**20)


def body(halves, first_factor, second_factor, weights):
    y_count, row_count = lax.axis_size("y"), lax.axis_size("p") * 2
    orbitals = halves.shape[0]
    block, virtual = first_factor.shape
    columns = 2 * y_count
    local = orbitals // columns
    column, core = lax.axis_index(("y", "zh")), lax.axis_index("c")

    lanes = (block + LANES - 1) // LANES * LANES
    half = virtual + orbitals // 2
    share = pl.pallas_call(
        pack_kernel,
        in_specs=SMEM + hbm(3),
        out_specs=vmem(1)[0],
        out_shape=jax.ShapeDtypeStruct((half, lanes), BF16),
        scratch_shapes=[pltpu.VMEM((half, block), BF16), pltpu.SemaphoreType.DMA((2,))],
        compiler_params=FULL,
        name="pack",
    )(core.reshape(1), first_factor.T, weights.T, second_factor.T)
    factors = lax.all_gather(share, ("y", "c"), axis=0, tiled=True).reshape(y_count, 2 * half, lanes)

    height = (ROWS + FOLD + 7) // 8 * 8
    split = halves.reshape(columns, local, ROWS, 2, ROWS).transpose(0, 3, 2, 1, 4)
    split = jnp.pad(split, ((0, 0),) * 4 + ((0, SLOT - ROWS),))
    four = split[:, :, :, :4].reshape(columns, 2, ROWS, LANES)
    two = split[:, :, :, 4:].reshape(columns, 2, ROWS, LANES // 2)
    fold = jnp.pad(two[:, :, FOLD:], ((0, 0), (0, 0), (0, 2 * FOLD - ROWS), (0, 0)))
    two = jnp.concatenate([two[:, :, :FOLD], fold], 3)
    spare = jnp.zeros((columns, 2, height - ROWS - FOLD, LANES), BF16)
    pieces = jnp.concatenate([four, two, spare], 2)
    direct = lax.all_to_all(pieces, ("y", "zh"), 0, 0, tiled=True).reshape(row_count, height, LANES)
    mirrored = lax.all_to_all(direct, ("p", "c"), 0, 0, tiled=True)
    slots, rows = local * SLOT, local * ROWS
    direct = pl.pallas_call(
        direct_kernel,
        in_specs=vmem(1),
        out_specs=vmem(1)[0],
        out_shape=jax.ShapeDtypeStruct((slots, virtual), BF16),
        scratch_shapes=[pltpu.VMEM((slots, row_count * SLOT), F32), pltpu.VMEM((row_count * SLOT, virtual), BF16)],
        compiler_params=ROOM,
        cost_estimate=pl.CostEstimate(flops=2 * slots * row_count * SLOT * virtual, bytes_accessed=4 * slots * virtual, transcendentals=0),
        name="direct",
    )(direct)
    packed = jax.ShapeDtypeStruct((packed_height(rows // 2, virtual)[-1], LANES), BF16)
    ours, front, back = pl.pallas_call(
        amplitude_kernel,
        in_specs=vmem(2),
        out_specs=vmem(3),
        out_shape=[jax.ShapeDtypeStruct((rows, virtual), BF16), packed, packed],
        scratch_shapes=[pltpu.VMEM((2, virtual, LANES), F32)],
        compiler_params=ROOM,
        name="amplitude",
    )(direct, mirrored)

    ready = pl.pallas_call(
        ready_kernel,
        in_specs=vmem(1),
        out_specs=vmem(1)[0],
        out_shape=jax.ShapeDtypeStruct((16, LANES), BF16),
        compiler_params=FETCH,
        cost_estimate=pl.CostEstimate(flops=0, bytes_accessed=2 * factors.size, transcendentals=0),
        name="ready",
    )(factors)

    def contraction(name, first, amplitude, result):
        return pl.pallas_call(
            functools.partial(
                contraction_kernel, orbitals=orbitals, rows=rows // 2 if result is packed else rows, depth=virtual, packed=result is packed, chunks=max(y_count // 2, 1)
            ),
            in_specs=SMEM + vmem(3),
            out_specs=vmem(1)[0],
            out_shape=result,
            compiler_params=BIG,
            cost_estimate=pl.CostEstimate(flops=rows * virtual * block * y_count * 4, bytes_accessed=y_count * 4 * half * lanes, transcendentals=0),
            name=name,
        )(first.reshape(1), amplitude, factors, ready)

    swap = [(0, 1), (1, 0)]
    partner = column + 1 - 2 * lax.axis_index("zh")
    theirs = [lax.ppermute(part, "zh", swap) for part in (front, back)]
    received = [
        lax.ppermute(contraction(f"contraction_sent_{k}", partner * local + k * (local // 2), theirs[k], packed), "zh", swap)
        for k in range(2)
    ]
    chunks = max(y_count // 2, 1)
    kept = pl.pallas_call(
        functools.partial(streamed_kernel, orbitals=orbitals, rows=rows, depth=virtual, packed=False),
        in_specs=SMEM + vmem(1) + hbm(1),
        out_specs=vmem(1)[0],
        out_shape=jax.ShapeDtypeStruct((rows, virtual), F32),
        scratch_shapes=[pltpu.VMEM((y_count, 2 * half, lanes), BF16), pltpu.SemaphoreType.DMA((chunks,))],
        compiler_params=pltpu.CompilerParams(vmem_limit_bytes=48 * 2**20),
        cost_estimate=pl.CostEstimate(flops=rows * virtual * block * y_count * 4, bytes_accessed=y_count * 4 * half * lanes, transcendentals=0),
        name="contraction_kept",
    )((column * local).reshape(1), ours, factors)
    return pl.pallas_call(
        finish_kernel,
        in_specs=vmem(3),
        out_specs=vmem(1)[0],
        out_shape=jax.ShapeDtypeStruct((local, ROWS, virtual), BF16),
        compiler_params=SMALL,
        name="finish",
    )(kept, *received)


def solution(mesh):
    rows, columns = mesh.devices.shape
    fine = Mesh(mesh.devices.reshape(rows // 2, 2, columns // 2, 2), ("p", "c", "y", "zh"))
    row, col = ("p", "c"), ("y", "zh")
    placed = (P(None, row, col), P(col, None), P(col, None), P(col, None))
    return jax.shard_map(body, mesh=fine, in_specs=placed, out_specs=P(col, row, None), check_vma=False)
```
